128 devices in a mesh: tm: 8 (over x, core), tile: 16 (over z, y).
Axes of the slice: x: 4, y: 4, z: 4, core: 2. Of those that a mesh axis runs over, the one named last changes fastest.
Arguments:
- basis: float32 [256, 256, 512], P(None, 'tile'), may hold values from -6 to 6
- diffusion: float32 [8, 256, 512], P('tm', 'tile'), may hold values from 0.12 to 0.24
- drift_x: float32 [8, 256, 512], P('tm', 'tile'), may hold values from -1 to 1
- drift_y: float32 [8, 256, 512], P('tm', 'tile'), may hold values from -1 to 1
- land_sea: int32 [256, 512], P('tile'), may hold values from 0 to 1, as said below
- obs_cells: int32 [8, 512], P('tm'), may hold values from 0 to 131071
- obs_values: float32 [8, 512], P('tm'), may hold values from -72 to 72
Outputs:
- group_coeffs: float32 [8, 2, 256], P('tm')
- end_fields: float32 [8, 256, 512], P('tm', 'tile')
The draws below stay inside these ranges and needn't reach their ends.
Inputs may be any that keep to these rules, and one draw needn't show every extreme that they name: `land_sea`: only 0 and 1; both occur. `obs_cells`: cells may repeat within and across groups.
All inputs are finite; a program needn't handle non-finite values.
Results may differ from the reference program's by a relative error of at most 0.0003.
Values sent between devices are 32-bit elements; how exact they have to be, the bound alone decides.
No kernel may reach another device: no remote copies, remote signals or barrier semaphores. Data moves between devices by JAX's collectives and lax.ppermute only.
A program may use at most 128 MiB of HBM per device.

```python
import math
import jax
import jax.numpy as jnp
from jax import lax

K = 256
STEPS = 6
NY = 512
NOBS = 512
NX = 256
G = 8


spread_rows = 1.0


spread_columns = 0.5


reach_cells = 6


island_count = 10


def smooth_weights(spread_value):
    raw = [math.exp(-0.5 * ((offset - reach_cells) / spread_value) ** 2) for offset in range(2 * reach_cells + 1)]
    norm_value = math.sqrt(sum((value * value for value in raw)))
    return [value / norm_value for value in raw]


def smooth_along(values, axis, spread_value):
    weights = smooth_weights(spread_value)
    length = values.shape[axis]
    padded = jnp.concatenate([lax.slice_in_dim(values, length - reach_cells, length, axis=axis), values, lax.slice_in_dim(values, 0, reach_cells, axis=axis)], axis=axis)
    summed = jnp.zeros_like(values)
    for position in range(2 * reach_cells + 1):
        summed = summed + weights[position] * lax.slice_in_dim(padded, position, position + length, axis=axis)
    return summed


def draw_basis(key, part):
    noise = jax.random.normal(key, (K, NX, NY), jnp.float32)
    smoothed = smooth_along(smooth_along(noise, 1, spread_rows), 2, spread_columns)
    return jnp.clip(smoothed, -6.0, 6.0).astype(jnp.float32)


def draw_drift_x(key, part):
    magnitude = jax.random.uniform(key, (G, NX, NY), jnp.float32, 0.7, 1.0)
    signs = (2 * jax.random.randint(jax.random.fold_in(key, 3), (G, 1, 1), 0, 2) - 1).astype(jnp.float32)
    return (magnitude * signs).astype(jnp.float32)


def draw_land_sea(key, part):
    keys = jax.random.split(key, 4)
    shape = (island_count, 1, 1)
    top_row = jax.random.randint(keys[0], shape, 0, NX)
    height = jax.random.randint(keys[1], shape, max(1, NX // 16), NX // 4 + 1)
    first_column = jax.random.randint(keys[2], shape, 0, NY)
    breadth = jax.random.randint(keys[3], shape, max(1, NY // 16), NY // 4 + 1)
    row_ids = jnp.arange(NX, dtype=jnp.int32)[None, :, None]
    column_ids = jnp.arange(NY, dtype=jnp.int32)[None, None, :]
    inside = (row_ids >= top_row) & (row_ids < top_row + height) & (column_ids >= first_column) & (column_ids < first_column + breadth)
    return (1 - jnp.any(inside, axis=0).astype(jnp.int32)).astype(jnp.int32)


def place_ends(drawn, own_key, least, largest):
    spot = [jax.random.randint(jax.random.fold_in(own_key, axis), (), 0, length) for axis, length in enumerate(drawn.shape)]
    longest = drawn.shape.index(max(drawn.shape))
    neighbour = spot[:longest] + [(spot[longest] + 1) % drawn.shape[longest]] + spot[longest + 1:]
    return drawn.at[tuple(spot)].set(least).at[tuple(neighbour)].set(largest)


def level_of(own_key, shape, shards, low, largest):
    def one(dim, shards_of):
        draws = jax.random.uniform(jax.random.fold_in(jax.random.fold_in(own_key, 6), dim), (shards_of,), jnp.float32, low / len(shards), largest / len(shards))
        return jnp.repeat(jnp.exp(draws), shape[dim] // shards_of).reshape((-1,) + (1,) * (len(shape) - dim - 1))

    loudness = one(*shards[0])
    for cut in shards[1:]:
        loudness = loudness * one(*cut)
    return loudness


def bell_draw(rng, dims, deviation, reach, shards=(), kind=jnp.bfloat16):
    factor_of = level_of(rng, dims, shards, -0.22, 0.18) if shards else 1.0
    entries = jax.random.normal(rng, dims, jnp.float32) * deviation * factor_of
    return jnp.minimum(jnp.maximum(entries, -reach), reach).astype(kind)


def setup_inputs(seed: int = 0) -> dict:
    splits = jax.random.split(jax.random.key(seed), 8)
    basis = draw_basis(jax.random.fold_in(splits[7], 71), 0)
    diffusion = jnp.clip(0.12 + 0.12 * jax.random.uniform(splits[1], (G, NX, NY), jnp.float32) ** level_of(splits[1], (G, NX, NY), ((0, 8), (1, 16)), -0.2, 0.2), 0.12, 0.24)
    drift_x = draw_drift_x(jax.random.fold_in(splits[7], 71), 0)
    drift_y = jnp.clip(jax.random.uniform(splits[3], (G, NX, NY), jnp.float32, -1.0, 1.0) * level_of(splits[3], (G, NX, NY), ((0, 8), (1, 16)), -0.4, 0.0), -1.0, 1.0)
    land_sea = draw_land_sea(jax.random.fold_in(splits[7], 71), 0)
    obs_cells = place_ends(jax.random.randint(splits[5], (G, NOBS), 0, NX * NY), jax.random.fold_in(splits[5], 1), 0, (NX * NY) - 1).astype(jnp.int32)
    obs_values = bell_draw(splits[6], (G, NOBS), 12.0, 72.0, ((0, 8),), jnp.float32)
    return dict(basis=basis, diffusion=diffusion, drift_x=drift_x, drift_y=drift_y, land_sea=land_sea, obs_cells=obs_cells, obs_values=obs_values)


q_inverse = 10.0
ridge = 0.1

def precise_dot(first, second):
    return jnp.dot(first, second, precision=lax.Precision.HIGHEST)

def group_terms(basis, sea_mask, inputs):
    diffusion, drift_x, drift_y, cells, values = inputs
    center_gain = 1.0 - 4.0 * diffusion
    east_gain = diffusion * (1.0 - drift_x)
    west_gain = diffusion * (1.0 + drift_x)
    north_gain = diffusion * (1.0 - drift_y)
    south_gain = diffusion * (1.0 + drift_y)
    field = basis
    for section in range(STEPS):
        padded_x = jnp.pad(field, ((0, 0), (1, 1), (0, 0)))
        padded_y = jnp.pad(field, ((0, 0), (0, 0), (1, 1)))
        field = sea_mask * (center_gain * field + east_gain * padded_x[:, 2:] + west_gain * padded_x[:, :-2] + north_gain * padded_y[:, :, 2:] + south_gain * padded_y[:, :, :-2])
    flat_basis = basis.reshape(K, NX * NY)
    propagator = precise_dot(flat_basis, field.reshape(K, NX * NY).T) / jnp.float32(NX * NY)
    obs_rows = jnp.take(flat_basis, cells, axis=1)
    obs_info = precise_dot(obs_rows, obs_rows.T) / jnp.float32(NOBS)
    obs_rhs = precise_dot(obs_rows, values) / jnp.float32(NOBS)
    return (propagator, obs_info, obs_rhs)

def reference(basis, diffusion, drift_x, drift_y, land_sea, obs_cells, obs_values):
    sea_mask = land_sea.astype(jnp.float32)
    propagators, infos, rhs_terms = lax.map(lambda inputs: group_terms(basis, sea_mask, inputs), (diffusion, drift_x, drift_y, obs_cells, obs_values))
    order = (G + 1) * K
    system = jnp.zeros((order, order), jnp.float32)
    right = jnp.zeros((order,), jnp.float32)
    identity = jnp.eye(K, dtype=jnp.float32)
    for group in range(G):
        prop = propagators[group]
        upper = q_inverse * precise_dot(prop.T, prop) + ridge * identity
        cross = -q_inverse * prop.T
        lower = (q_inverse + ridge) * identity + infos[group]
        start = group * K
        system = system.at[start:start + K, start:start + K].add(upper)
        system = system.at[start:start + K, start + K:start + 2 * K].add(cross)
        system = system.at[start + K:start + 2 * K, start:start + K].add(cross.T)
        system = system.at[start + K:start + 2 * K, start + K:start + 2 * K].add(lower)
        right = right.at[start + K:start + 2 * K].add(rhs_terms[group])
    states = jnp.linalg.solve(system, right).reshape(G + 1, K)
    group_coeffs = jnp.stack([states[:-1], states[1:]], axis=1)
    end_fields = jnp.tensordot(states[1:], basis, axes=1, precision=lax.Precision.HIGHEST)
    return (group_coeffs, end_fields)
```

```python
import functools

import jax
import jax.numpy as jnp
from jax import lax
from jax.experimental import pallas as pl
from jax.experimental.pallas import tpu as pltpu
from jax.sharding import PartitionSpec as P

STEPS = 6
REACH = STEPS // 2
NOBS = 512
Q = 10.0
RIDGE = 0.1
SUB = 8
LANES = 128
SLICE = 40
TAIL = 8


def split(value):
    high = value.astype(jnp.bfloat16)
    low = (value - high.astype(jnp.float32)).astype(jnp.bfloat16)
    return high, low


def dot3(left, right):
    lh, ll = split(left)
    rh, rl = split(right)
    return lax.dot_general(
        jnp.concatenate([lh, lh, ll], axis=1),
        jnp.concatenate([rh, rl, rh], axis=1),
        (((1,), (1,)), ((), ())),
        preferred_element_type=jnp.float32,
    )


def full(left, right, contract=(1, 0)):
    return lax.dot_general(
        left,
        right,
        (((contract[0],), (contract[1],)), ((), ())),
        precision=lax.Precision.HIGHEST,
        preferred_element_type=jnp.float32,
    )


def deal_matrix(columns, copies):
    strips = columns // LANES
    source = lax.broadcasted_iota(jnp.int32, (columns, columns), 0)
    target = lax.broadcasted_iota(jnp.int32, (columns, columns), 1)
    wanted = (target % LANES) * strips + target // LANES
    one = jnp.where(source == wanted, 1.0, 0.0).astype(jnp.bfloat16)
    return jnp.concatenate([one] * copies, axis=0)


def dealt(value, deal):
    parts, rest = [], value
    for _ in range(deal.shape[0] // deal.shape[1]):
        part = rest.astype(jnp.bfloat16)
        parts.append(part)
        rest = rest - part.astype(jnp.float32)
    return jnp.dot(jnp.concatenate(parts, axis=1), deal, preferred_element_type=jnp.float32)


def strips_of(value):
    return [value[:, c : c + LANES] for c in range(0, value.shape[1], LANES)]


def after(strips):
    return strips[1:] + [pltpu.roll(strips[0], LANES - 1, 1)]


def before(strips):
    return [pltpu.roll(strips[-1], 1, 1)] + strips[:-1]


def lay_kernel(rows, count_ref, value_ref, *refs):
    basis_refs, (field_ref, out_ref, deal, held) = refs[:-4], refs[-4:]
    step_id = pl.program_id(0)
    width = held.shape[1]
    block = basis_refs[0].shape[0] // rows

    @pl.when(step_id == 0)
    def _():
        deal[...] = deal_matrix(deal.shape[1], 2)

    lines = []
    for i in range(rows):
        span = pl.ds(i, block, stride=rows)
        lines.append(jnp.concatenate([ref[span, :] for ref in basis_refs], axis=1))
    laid = dealt(jnp.concatenate(lines, axis=0), deal[...])
    at = pl.ds(pl.multiple_of(step_id * block, block), block)
    for i in range(rows):
        line = laid[i * block : (i + 1) * block]
        field_ref[i] = line
        held[i, at, :] = line

    @pl.when(step_id == pl.num_programs(0) - 1)
    def _():
        out_ref[...] = jnp.zeros_like(out_ref)

        def body(i, carry):
            field = held[i]
            count = count_ref[pl.ds(i, 1), :]
            value = jnp.broadcast_to(value_ref[pl.ds(i, 1), :], (TAIL, count.shape[1]))
            out_ref[...] += dot3(jnp.concatenate([field * count, value], axis=0), field)
            return carry

        lax.fori_loop(0, rows, body, 0)


def lay_basis(basis2, count, value, width, rows):
    columns = basis2.shape[1]
    block = 32
    strips = columns // LANES
    return pl.pallas_call(
        functools.partial(lay_kernel, rows),
        grid=(width // block,),
        in_specs=[
            pl.BlockSpec((rows, columns), lambda k: (0, 0)),
            pl.BlockSpec((rows, columns), lambda k: (0, 0)),
            *[pl.BlockSpec((block * rows, LANES), lambda k, c=c: (k, c)) for c in range(strips)],
        ],
        out_specs=[
            pl.BlockSpec((rows, block, columns), lambda k: (0, k, 0)),
            pl.BlockSpec((width + TAIL, width), lambda k: (0, 0)),
        ],
        out_shape=[
            jax.ShapeDtypeStruct((rows, width, columns), jnp.float32),
            jax.ShapeDtypeStruct((width + TAIL, width), jnp.float32),
        ],
        scratch_shapes=[
            pltpu.VMEM((2 * columns, columns), jnp.bfloat16),
            pltpu.VMEM((rows, width, columns), jnp.float32),
        ],
        name="lay_basis",
    )(count, value, *[basis2] * strips)


def prop_kernel(
    place_ref, model_ref, field_ref, low_mine, low_theirs, high_mine, high_theirs, obs_ref,
    out_ref, deal, model, wide, edges, fore, back,
):
    step_id = pl.program_id(0)
    steps = pl.num_programs(0)
    rows, block, columns = field_ref.shape
    ext = rows + 2 * REACH
    width = fore.shape[1]
    half = width // 2
    core, tile, last_tile = place_ref[0], place_ref[1], place_ref[2]
    turn = lax.rem(step_id + core * (steps // 2), steps)

    @pl.when(step_id == 0)
    def _():
        deal[...] = deal_matrix(columns, 3)
        model[...] = jnp.zeros_like(model)
        for f in range(4):
            for r in range(REACH):
                model[f, r : r + 1, :] = low_mine[r, half + f : half + f + 1, :]
                at = REACH + rows + r
                model[f, at : at + 1, :] = high_mine[r, half + f : half + f + 1, :]
            for r in range(rows):
                model[f, REACH + r : REACH + r + 1, :] = model_ref[f, r : r + 1, :]
        tall = model.shape[1]
        together = dealt(model[...].reshape(4 * tall, columns), deal[...])
        lines = lax.broadcasted_iota(jnp.int32, (tall, LANES), 0)
        lanes = lax.broadcasted_iota(jnp.int32, (tall, LANES), 1)
        no_west = jnp.logical_and(tile == 0, lines == REACH)
        no_east = jnp.logical_and(tile == last_tile, lines == REACH + rows - 1)
        diffusion, drift_x, drift_y, sea = (
            strips_of(together[f * tall : (f + 1) * tall]) for f in range(4)
        )
        center, east, west, north, south = [], [], [], [], []
        for c in range(len(sea)):
            center.append(sea[c] * (1.0 - 4.0 * diffusion[c]))
            east.append(jnp.where(no_east, 0.0, sea[c] * (diffusion[c] * (1.0 - drift_x[c]))))
            west.append(jnp.where(no_west, 0.0, sea[c] * (diffusion[c] * (1.0 + drift_x[c]))))
            up = sea[c] * (diffusion[c] * (1.0 - drift_y[c]))
            down = sea[c] * (diffusion[c] * (1.0 + drift_y[c]))
            if c == len(sea) - 1:
                up = jnp.where(lanes == LANES - 1, 0.0, up)
            if c == 0:
                down = jnp.where(lanes == 0, 0.0, down)
            north.append(up)
            south.append(down)
        sets = (
            (center, 0), (east, 0), (west, 0), (north, 0), (south, 0),
            (west, 1), (east, -1), (after(south), 0), (before(north), 0),
        )
        for g, (values, move) in enumerate(sets):
            for r in range(ext):
                if not 0 <= r + move < ext:
                    continue
                line = jnp.concatenate([v[r + move : r + move + 1] for v in values], axis=1)
                wide[g * ext + r] = jnp.broadcast_to(line, (SUB, columns))

    def deal_edges(low, high):
        count = REACH * half
        low_rows = low[:, :half, :].reshape(count, columns)
        high_rows = high[:, :half, :].reshape(count, columns)
        twice = deal[: 2 * columns, :]
        edges[:REACH] = dealt(low_rows, twice).reshape(REACH, half, columns)
        edges[REACH:] = dealt(high_rows, twice).reshape(REACH, half, columns)

    @pl.when(step_id == 0)
    def _():
        deal_edges(low_mine, high_mine)

    @pl.when(step_id == steps // 2)
    def _():
        deal_edges(low_theirs, high_theirs)

    def one(kt, carry):
        near = pl.ds(pl.multiple_of(kt * SUB, SUB), SUB)
        edge = pl.ds(pl.multiple_of(lax.rem(step_id, steps // 2) * block + kt * SUB, SUB), SUB)
        store = pl.ds(pl.multiple_of(turn * block + kt * SUB, SUB), SUB)

        def start(i):
            if i < 0:
                return strips_of(edges[i + REACH, edge, :])
            if i >= rows:
                return strips_of(edges[i - rows + REACH, edge, :])
            return strips_of(field_ref[i, near, :])

        for target, sets in ((fore, (0, 1, 2, 3, 4)), (back, (0, 5, 6, 7, 8))):
            levels = [{} for _ in range(REACH + 1)]
            for lead in range(-REACH, rows + REACH):
                levels[0][lead] = start(lead)
                for s in range(1, REACH + 1):
                    i = lead - s
                    if -REACH + s <= i < rows + REACH - s:
                        prev = levels[s - 1]
                        gains = [wide[g * ext + i + REACH] for g in sets]
                        shifted = (
                            prev[i], prev[i + 1], prev[i - 1], after(prev[i]), before(prev[i])
                        )
                        levels[s][i] = []
                        for c in range(columns // LANES):
                            terms = [
                                gain[:, c * LANES : (c + 1) * LANES] * value[c]
                                for gain, value in zip(gains, shifted)
                            ]
                            levels[s][i].append(
                                (terms[0] + (terms[1] + terms[2])) + (terms[3] + terms[4])
                            )
                i = lead - REACH
                if 0 <= i < rows:
                    target[i, store, :] = jnp.concatenate(levels[REACH][i], axis=1)
        return carry

    lax.fori_loop(0, block // SUB, one, 0)

    @pl.when(step_id == steps - 1)
    def _():
        count = out_ref.shape[0]
        part = width // count

        def body(i, carry):
            product = dot3(back[i], fore[i])
            fresh = i == 0
            for t in range(count):
                piece = product[t * part : (t + 1) * part]
                out_ref[t, :part, :] = jnp.where(fresh, 0.0, out_ref[t, :part, :]) + piece
            return carry

        lax.fori_loop(0, rows, body, 0)
        for t in range(count):
            out_ref[t, part : 2 * part, :] = obs_ref[t * part : (t + 1) * part, :]
            out_ref[t, 2 * part :, :] = obs_ref[width : width + SLICE - 2 * part, :]


def prop_terms(place, model, field, edges, obs, count):
    rows, width, columns = field.shape
    block = 32
    steps = width // block
    ext = rows + 2 * REACH
    vmem = pl.BlockSpec(memory_space=pltpu.VMEM)
    return pl.pallas_call(
        prop_kernel,
        grid_spec=pltpu.PrefetchScalarGridSpec(
            num_scalar_prefetch=1,
            grid=(steps,),
            in_specs=[
                vmem,
                pl.BlockSpec(
                    (rows, block, columns),
                    lambda k, place: (0, lax.rem(k + place[0] * (steps // 2), steps), 0),
                ),
                vmem,
                vmem,
                vmem,
                vmem,
                vmem,
            ],
            out_specs=pl.BlockSpec((count, SLICE, width), lambda k, place: (0, 0, 0)),
            scratch_shapes=[
                pltpu.VMEM((3 * columns, columns), jnp.bfloat16),
                pltpu.VMEM((4, -(-ext // SUB) * SUB, columns), jnp.float32),
                pltpu.VMEM((9 * ext, SUB, columns), jnp.float32),
                pltpu.VMEM((2 * REACH, width // 2, columns), jnp.float32),
                pltpu.VMEM((rows, width, columns), jnp.float32),
                pltpu.VMEM((rows, width, columns), jnp.float32),
            ],
        ),
        out_shape=jax.ShapeDtypeStruct((count, SLICE, width), jnp.float32),
        name="prop_terms",
    )(place, model, field, *edges, obs)


def eye_mask(width):
    row = lax.broadcasted_iota(jnp.int32, (width, width), 0)
    col = lax.broadcasted_iota(jnp.int32, (width, width), 1)
    return row, col


def product(left, right, passes):
    if passes == 1:
        return jnp.dot(
            left.astype(jnp.bfloat16),
            right.astype(jnp.bfloat16),
            preferred_element_type=jnp.float32,
        )
    if passes == 3:
        lh, ll = split(left)
        rh, rl = split(right)
        return jnp.dot(
            jnp.concatenate([lh, lh, ll], axis=1),
            jnp.concatenate([rh, rl, rh], axis=0),
            preferred_element_type=jnp.float32,
        )
    return full(left, right)


def inverses(mats):
    width = mats[0].shape[0]
    row, col = eye_mask(width)
    identity = jnp.where(row == col, 1.0, 0.0).astype(jnp.float32)
    guesses = []
    for mat in mats:
        bound = jnp.max(jnp.sum(jnp.abs(mat), axis=0, keepdims=True), axis=1, keepdims=True)
        guesses.append(identity * (1.7 / bound))

    def stage(state, passes, goal, slowest):
        def more(state):
            turn, error, last = state[0], state[1], state[2]
            going = jnp.logical_and(error > goal, turn < 100)
            return jnp.logical_and(going, jnp.logical_or(error < slowest * last, last == 0.0))

        def improve(state):
            error = jnp.float32(0.0)
            found = []
            for mat, guess in zip(mats, state[3:]):
                rest = identity - product(mat, guess, passes[0])
                found.append(guess + product(guess, rest, passes[1]))
                error = jnp.maximum(error, jnp.sum(rest * rest))
            return (state[0] + 1, error, state[1], *found)

        return lax.while_loop(more, improve, state)

    found = guesses
    turn = jnp.int32(0)
    large = jnp.float32(1e30)
    for passes, goal, slowest in (((1, 1), 2.0, 0.5), ((3, 1), 1e-3, 0.5), ((6, 3), 1e-6, 2.0)):
        state = stage((turn, large, jnp.float32(0.0), *found), passes, goal, slowest)
        turn, found = state[0], state[3:]
    return found


def pair_kernel(core_ref, own_ref, other_ref, both_ref, send_ref, left_ref, right_ref, mid_ref, prop, info):
    count, _, width = own_ref.shape
    part = width // count
    first = core_ref[0] == 0
    row, col = eye_mask(width)
    identity = jnp.where(row == col, 1.0, 0.0).astype(jnp.float32)
    for t in range(count):
        span = pl.ds(t * part, part)
        for slot, lead in ((0, True), (1, False)):
            mine, theirs = own_ref[t], other_ref[t]
            chosen = jnp.where(first, mine, theirs) if lead else jnp.where(first, theirs, mine)
            prop[slot, span, :] = chosen[:part]
            info[slot, span, :] = chosen[part : 2 * part]
    rhs_own, rhs_other = own_ref[0, 2 * part :, :], other_ref[0, 2 * part :, :]
    rhs_left = jnp.where(first, rhs_own, rhs_other)
    rhs_right = jnp.where(first, rhs_other, rhs_own)
    p_left, p_right = prop[0], prop[1]
    square_left = full(p_left, p_left, (0, 0))
    square_right = full(p_right, p_right, (0, 0))
    middle = (Q + 2 * RIDGE) * identity + info[0] + Q * square_right
    (back,) = inverses([middle])
    toward_left = full(p_left, back, (0, 0))
    toward_right = full(jnp.concatenate([p_right, rhs_left], axis=0), back)
    mid = toward_right[width:]
    toward_right = toward_right[:width]
    by_left = full(jnp.concatenate([toward_left, mid], axis=0), p_left)
    by_right = full(jnp.concatenate([toward_left, toward_right, mid], axis=0), p_right, (1, 1))
    upper = Q * square_left + RIDGE * identity - (Q * Q) * by_left[:width]
    cross = -(Q * Q) * by_right[:width]
    lower = (Q + RIDGE) * identity + info[1] - (Q * Q) * by_right[width : 2 * width]
    head = Q * by_left[width:]
    tail = rhs_right + Q * by_right[2 * width :]
    lower_diag = jnp.sum(jnp.where(row == col, lower, 0.0), axis=0, keepdims=True)
    both_ref[0, :width, :] = jnp.where(row >= col, upper, lower)
    small = lax.broadcasted_iota(jnp.int32, (TAIL, width), 0)
    both_ref[0, width:, :] = jnp.where(small == 0, lower_diag, jnp.where(small == 1, head, tail))
    both_ref[1, :width, :] = cross
    both_ref[1, width:, :] = jnp.zeros((TAIL, width), jnp.float32)
    send_ref[...] = jnp.where(first, both_ref[0], both_ref[1])
    left_ref[...] = Q * toward_left
    right_ref[...] = Q * toward_right
    mid_ref[...] = mid


def merge_pair(core, own, other):
    count, _, width = own.shape
    vmem = pl.BlockSpec(memory_space=pltpu.VMEM)
    block = jax.ShapeDtypeStruct((width, width), jnp.float32)
    return pl.pallas_call(
        pair_kernel,
        in_specs=[pl.BlockSpec(memory_space=pltpu.SMEM), vmem, vmem],
        out_specs=[vmem] * 5,
        out_shape=[
            jax.ShapeDtypeStruct((2, width + TAIL, width), jnp.float32),
            jax.ShapeDtypeStruct((width + TAIL, width), jnp.float32),
            block,
            block,
            jax.ShapeDtypeStruct((TAIL, width), jnp.float32),
        ],
        scratch_shapes=[pltpu.VMEM((2, width, width), jnp.float32)] * 2,
        name="merge_pair",
    )(core, own, other)


def chain_kernel(
    place_ref, both_ref, m_prev, o_prev, m_next, o_next, m_far, o_far, left_ref, right_ref, mid_ref,
    coeff_ref, blocks, states,
):
    core, chip = place_ref[0], place_ref[1]
    width = both_ref.shape[2]
    row, col = eye_mask(width)
    blocks[chip] = both_ref[...]
    for mine, theirs, move in ((m_prev, o_prev, 3), (m_next, o_next, 1), (m_far, o_far, 2)):
        at = lax.rem(chip + move, 4)
        blocks[at, core] = mine[...]
        blocks[at, 1 - core] = theirs[...]
    upper, lower, cross, head, tail = [], [], [], [], []
    for c in range(4):
        packed = blocks[c, 0, :width, :]
        turned = packed.T
        small = blocks[c, 0, width:, :]
        upper.append(jnp.where(row >= col, packed, turned))
        off = jnp.where(row < col, packed, turned)
        lower.append(jnp.where(row == col, jnp.broadcast_to(small[0:1], (width, width)), off))
        head.append(jnp.broadcast_to(small[1:2], (TAIL, width)))
        tail.append(jnp.broadcast_to(small[2:3], (TAIL, width)))
        cross.append(blocks[c, 1, :width, :])
    diag = [upper[0], lower[0] + upper[1], lower[1] + upper[2], lower[2] + upper[3], lower[3]]
    rhs = [head[0], tail[0] + head[1], tail[1] + head[2], tail[2] + head[3], tail[3]]
    inv0, inv2, inv4 = inverses([diag[0], diag[2], diag[4]])
    t10 = full(cross[0], inv0, (0, 0))
    t12 = full(cross[1], inv2)
    t32 = full(cross[2], inv2, (0, 0))
    t34 = full(cross[3], inv4)
    z0, z2, z4 = full(rhs[0], inv0), full(rhs[2], inv2), full(rhs[4], inv4)
    diag1 = diag[1] - full(t10, cross[0]) - full(t12, cross[1], (1, 1))
    diag3 = diag[3] - full(t32, cross[2]) - full(t34, cross[3], (1, 1))
    link = -full(t12, cross[2])
    rhs1 = rhs[1] - full(z0, cross[0]) - full(z2, cross[1], (1, 1))
    rhs3 = rhs[3] - full(z2, cross[2]) - full(z4, cross[3], (1, 1))
    (inv1,) = inverses([diag1])
    t31 = full(link, inv1, (0, 0))
    z1 = full(rhs1, inv1)
    diag3 = diag3 - full(t31, link)
    rhs3 = rhs3 - full(z1, link)
    (inv3,) = inverses([diag3])
    y3 = full(rhs3, inv3)
    y1 = z1 - full(y3, t31)
    y0 = z0 - full(y1, t10)
    y2 = z2 - full(y1, t12) - full(y3, t32)
    y4 = z4 - full(y3, t34)
    for c, state in enumerate((y0, y1, y2, y3, y4)):
        states[c] = state
    begin, finish = states[chip], states[chip + 1]
    inner = mid_ref[...] + full(begin, left_ref[...]) + full(finish, right_ref[...])
    first = core == 0
    start = jnp.where(first, begin, inner)
    end = jnp.where(first, inner, finish)
    pick = lax.broadcasted_iota(jnp.int32, (TAIL, width), 0)
    coeff_ref[...] = jnp.where(pick == 0, start, end)


def solve_chain(place, both, received, left, right, mid):
    width = both.shape[2]
    vmem = pl.BlockSpec(memory_space=pltpu.VMEM)
    return pl.pallas_call(
        chain_kernel,
        in_specs=[pl.BlockSpec(memory_space=pltpu.SMEM)] + [vmem] * 10,
        out_specs=vmem,
        out_shape=jax.ShapeDtypeStruct((TAIL, width), jnp.float32),
        scratch_shapes=[
            pltpu.VMEM((4, 2, width + TAIL, width), jnp.float32),
            pltpu.VMEM((5, TAIL, width), jnp.float32),
        ],
        name="solve_chain",
    )(place, both, *received, left, right, mid)


def shift(value, axis, step, wrap):
    size = lax.axis_size(axis)
    pairs = [(i, (i + step) % size) for i in range(size) if wrap or 0 <= i + step < size]
    return lax.ppermute(value, axis, pairs)


def swap_core(value):
    return lax.ppermute(value, "tm", [(i, i ^ 1) for i in range(lax.axis_size("tm"))])


def edge_rows(basis, model):
    width, rows, columns = basis.shape
    core = lax.axis_index("tm") & 1
    half = lax.dynamic_slice_in_dim(basis, core * (width // 2), width // 2, axis=0)
    half = jnp.concatenate([half, jnp.pad(model, ((0, TAIL - model.shape[0]), (0, 0), (0, 0)))], axis=0)
    low = shift(jnp.swapaxes(half[:, rows - REACH :], 0, 1), "tile", 1, False)
    high = shift(jnp.swapaxes(half[:, :REACH], 0, 1), "tile", -1, False)
    return low, swap_core(low), high, swap_core(high)


def obs_maps(cells, values, rows, columns):
    local = cells - lax.axis_index("tile") * (rows * columns)
    row = local // columns
    col = local & (columns - 1)
    strips = columns // LANES
    col = (col % strips) * LANES + col // strips
    by_row = (row[None, :] == jnp.arange(rows)[:, None]).astype(jnp.float32)
    by_col = (col[:, None] == jnp.arange(columns)[None, :]).astype(jnp.float32)
    both = jnp.concatenate([by_row, by_row * values[None, :]], axis=0)
    maps = jnp.dot(both, by_col, precision=lax.Precision.HIGHEST)
    return maps[:rows], maps[rows:]


def shards(basis, diffusion, drift_x, drift_y, land_sea, obs_cells, obs_values):
    width, rows, columns = basis.shape
    tiles = lax.axis_size("tile")
    group = lax.axis_index("tm")
    core = group & 1
    chip = group >> 1
    basis2 = basis.reshape(width * rows, columns)
    model = jnp.stack([diffusion[0], drift_x[0], drift_y[0], land_sea.astype(jnp.float32)])
    edges = edge_rows(basis, model)
    count, value = obs_maps(obs_cells[0], obs_values[0], rows, columns)
    field, obs = lay_basis(basis2, count, value, width, rows)
    place = jnp.stack([core, lax.axis_index("tile"), jnp.int32(tiles - 1)])
    partial = prop_terms(place, model, field, edges, obs, tiles)

    pieces = lax.all_to_all(partial, "tile", 0, 0, tiled=True)
    reduced = jnp.sum(pieces, axis=0)
    part = width // tiles
    lines = lax.broadcasted_iota(jnp.int32, reduced.shape, 0)
    scale = jnp.where(lines < part, 1.0 / float(tiles * rows * columns), 1.0 / float(NOBS))
    spread = jnp.broadcast_to((reduced * scale)[None], partial.shape)
    own = lax.all_to_all(spread, "tile", 0, 0, tiled=True)
    other = swap_core(own)

    both, send, left, right, mid = merge_pair(core[None], own, other)
    prev_mine = shift(send, "tm", 2, True)
    next_mine = shift(send, "tm", -2, True)
    size = lax.axis_size("tm")
    onward = [(i, (i + (2 if i % 2 == 0 else size - 2)) % size) for i in range(size)]
    far_mine = lax.ppermute(jnp.where(core == 0, prev_mine, next_mine), "tm", onward)
    received = []
    for mine in (prev_mine, next_mine, far_mine):
        received += [mine, swap_core(mine)]
    coeffs = solve_chain(jnp.stack([core, chip]), both, received, left, right, mid)
    group_coeffs = coeffs[:2][None]
    end_fields = jnp.sum(basis * coeffs[1][:, None, None], axis=0)[None]
    return (group_coeffs, end_fields)


def solution(mesh):
    in_specs = (
        P(None, "tile", None),
        P("tm", "tile", None),
        P("tm", "tile", None),
        P("tm", "tile", None),
        P("tile", None),
        P("tm", None),
        P("tm", None),
    )
    out_specs = (P("tm", None, None), P("tm", "tile", None))
    return jax.shard_map(shards, mesh=mesh, in_specs=in_specs, out_specs=out_specs, check_vma=False)
```

```python
import functools

import jax
import jax.numpy as jnp
from jax import lax
from jax.experimental import pallas as pl
from jax.experimental.pallas import tpu as pltpu
from jax.sharding import PartitionSpec as P

STEPS = 6
REACH = STEPS // 2
NOBS = 512
Q = 10.0
RIDGE = 0.1
SUB = 8
LANES = 128
TAIL = 8


def split(value):
    high = value.astype(jnp.bfloat16)
    low = (value - high.astype(jnp.float32)).astype(jnp.bfloat16)
    return high, low


def dot3(left, right):
    lh, ll = split(left)
    rh, rl = split(right)
    return lax.dot_general(
        jnp.concatenate([lh, lh, ll], axis=1),
        jnp.concatenate([rh, rl, rh], axis=1),
        (((1,), (1,)), ((), ())),
        preferred_element_type=jnp.float32,
    )


def dot(left, right, contract=(1, 0)):
    lh, ll = split(left)
    rh, rl = split(right)
    return lax.dot_general(
        jnp.concatenate([lh, lh, ll], axis=contract[0]),
        jnp.concatenate([rh, rl, rh], axis=contract[1]),
        (((contract[0],), (contract[1],)), ((), ())),
        preferred_element_type=jnp.float32,
    )


def deal_matrix(columns, copies):
    strips = columns // LANES
    source = lax.broadcasted_iota(jnp.int32, (columns, columns), 0)
    target = lax.broadcasted_iota(jnp.int32, (columns, columns), 1)
    wanted = (target % LANES) * strips + target // LANES
    one = jnp.where(source == wanted, 1.0, 0.0).astype(jnp.bfloat16)
    return jnp.concatenate([one] * copies, axis=0)


def dealt(value, deal):
    parts, rest = [], value
    for _ in range(deal.shape[0] // deal.shape[1]):
        part = rest.astype(jnp.bfloat16)
        parts.append(part)
        rest = rest - part.astype(jnp.float32)
    return jnp.dot(jnp.concatenate(parts, axis=1), deal, preferred_element_type=jnp.float32)


def strips_of(value):
    return [value[:, c : c + LANES] for c in range(0, value.shape[1], LANES)]


def after(strips):
    return strips[1:] + [pltpu.roll(strips[0], LANES - 1, 1)]


def before(strips):
    return [pltpu.roll(strips[-1], 1, 1)] + strips[:-1]


def edge_kernel(rows, core_ref, *refs):
    model_refs, basis_refs, (low_ref, high_ref, model_ref) = refs[:4], refs[4:-3], refs[-3:]
    step_id = pl.program_id(0)
    block = basis_refs[0].shape[0] // rows
    half = low_ref.shape[1] - TAIL

    @pl.when(step_id == 0)
    def _():
        for f, ref in enumerate(model_refs):
            model_ref[f] = ref[0].astype(jnp.float32)
        for r in range(REACH):
            low_ref[r, half:, :] = jnp.zeros_like(low_ref[r, half:, :])
            high_ref[r, half:, :] = jnp.zeros_like(high_ref[r, half:, :])
            for f in range(4):
                at = rows - REACH + r
                low_ref[r, half + f : half + f + 1, :] = model_ref[f, at : at + 1, :]
                high_ref[r, half + f : half + f + 1, :] = model_ref[f, r : r + 1, :]

    store = pl.ds(pl.multiple_of(step_id * block, block), block)
    for r in range(REACH):
        for out, i in ((low_ref, rows - REACH + r), (high_ref, r)):
            span = pl.ds(i, block, stride=rows)
            out[r, store, :] = jnp.concatenate([ref[span, :] for ref in basis_refs], axis=1)


def edge_terms(core, models, basis2, width, rows):
    columns = basis2.shape[1]
    block = 32
    strips = columns // LANES
    steps = width // 2 // block
    own = pl.BlockSpec((1, rows, columns), lambda k, core: (0, 0, 0))
    edge = (REACH, width // 2 + TAIL, columns)
    return pl.pallas_call(
        functools.partial(edge_kernel, rows),
        grid_spec=pltpu.PrefetchScalarGridSpec(
            num_scalar_prefetch=1,
            grid=(steps,),
            in_specs=[own] * 4
            + [
                pl.BlockSpec((block * rows, LANES), lambda k, core, c=c: (k + core[0] * steps, c))
                for c in range(strips)
            ],
            out_specs=[
                pl.BlockSpec(edge, lambda k, core: (0, 0, 0)),
                pl.BlockSpec(edge, lambda k, core: (0, 0, 0)),
                pl.BlockSpec((4, rows, columns), lambda k, core: (0, 0, 0)),
            ],
        ),
        out_shape=[
            jax.ShapeDtypeStruct(edge, jnp.float32),
            jax.ShapeDtypeStruct(edge, jnp.float32),
            jax.ShapeDtypeStruct((4, rows, columns), jnp.float32),
        ],
        name="edge_terms",
    )(core, *models, *[basis2] * strips)


def lay_kernel(rows, count_ref, value_ref, *refs):
    basis_refs, (field_ref, out_ref, deal, held) = refs[:-4], refs[-4:]
    step_id = pl.program_id(0)
    width = held.shape[1]
    block = basis_refs[0].shape[0] // rows

    @pl.when(step_id == 0)
    def _():
        deal[...] = deal_matrix(deal.shape[1], 2)

    lines = []
    for i in range(rows):
        span = pl.ds(i, block, stride=rows)
        lines.append(jnp.concatenate([ref[span, :] for ref in basis_refs], axis=1))
    laid = dealt(jnp.concatenate(lines, axis=0), deal[...])
    at = pl.ds(pl.multiple_of(step_id * block, block), block)
    for i in range(rows):
        line = laid[i * block : (i + 1) * block]
        field_ref[i] = line
        held[i, at, :] = line

    @pl.when(step_id == pl.num_programs(0) - 1)
    def _():
        out_ref[...] = jnp.zeros_like(out_ref)
        tiles = out_ref.shape[0]
        part = width // tiles

        def body(i, carry):
            field = held[i]
            count = count_ref[pl.ds(i, 1), :]
            value = jnp.broadcast_to(value_ref[pl.ds(i, 1), :], (TAIL, count.shape[1]))
            terms = dot3(jnp.concatenate([field * count, value], axis=0), field)
            for t in range(tiles):
                out_ref[t, :part, :] += terms[t * part : (t + 1) * part]
            out_ref[0, part:, :] += terms[width:]
            return carry

        lax.fori_loop(0, rows, body, 0)


def lay_basis(basis2, count, value, width, rows, tiles):
    columns = basis2.shape[1]
    block = 32
    strips = columns // LANES
    return pl.pallas_call(
        functools.partial(lay_kernel, rows),
        grid=(width // block,),
        in_specs=[
            pl.BlockSpec((rows, columns), lambda k: (0, 0)),
            pl.BlockSpec((rows, columns), lambda k: (0, 0)),
            *[pl.BlockSpec((block * rows, LANES), lambda k, c=c: (k, c)) for c in range(strips)],
        ],
        out_specs=[
            pl.BlockSpec((rows, block, columns), lambda k: (0, k, 0)),
            pl.BlockSpec((tiles, width // tiles + TAIL, width), lambda k: (0, 0, 0)),
        ],
        out_shape=[
            jax.ShapeDtypeStruct((rows, width, columns), jnp.float32),
            jax.ShapeDtypeStruct((tiles, width // tiles + TAIL, width), jnp.float32),
        ],
        scratch_shapes=[
            pltpu.VMEM((2 * columns, columns), jnp.bfloat16),
            pltpu.VMEM((rows, width, columns), jnp.float32),
        ],
        cost_estimate=pl.CostEstimate(flops=20 * 10**9, bytes_accessed=17 * 10**6, transcendentals=0),
        name="lay_basis",
    )(count, value, *[basis2] * strips)


def prop_kernel(
    place_ref, model_ref, field_ref, low_mine, low_theirs, high_mine, high_theirs,
    out_ref, deal, model, wide, edges, fore, back,
):
    step_id = pl.program_id(0)
    steps = pl.num_programs(0)
    rows, block, columns = field_ref.shape
    ext = rows + 2 * REACH
    width = fore.shape[1]
    half = width // 2
    core, tile, last_tile = place_ref[0], place_ref[1], place_ref[2]
    turn = lax.rem(step_id + core * (steps // 2), steps)

    @pl.when(step_id == 0)
    def _():
        deal[...] = deal_matrix(columns, 3)
        model[...] = jnp.zeros_like(model)
        for f in range(4):
            for r in range(REACH):
                model[f, r : r + 1, :] = low_mine[r, half + f : half + f + 1, :]
                at = REACH + rows + r
                model[f, at : at + 1, :] = high_mine[r, half + f : half + f + 1, :]
            for r in range(rows):
                model[f, REACH + r : REACH + r + 1, :] = model_ref[f, r : r + 1, :]
        tall = model.shape[1]
        together = dealt(model[...].reshape(4 * tall, columns), deal[...])
        lines = lax.broadcasted_iota(jnp.int32, (tall, LANES), 0)
        lanes = lax.broadcasted_iota(jnp.int32, (tall, LANES), 1)
        no_west = jnp.logical_and(tile == 0, lines == REACH)
        no_east = jnp.logical_and(tile == last_tile, lines == REACH + rows - 1)
        diffusion, drift_x, drift_y, sea = (
            strips_of(together[f * tall : (f + 1) * tall]) for f in range(4)
        )
        center, east, west, north, south = [], [], [], [], []
        for c in range(len(sea)):
            center.append(sea[c] * (1.0 - 4.0 * diffusion[c]))
            east.append(jnp.where(no_east, 0.0, sea[c] * (diffusion[c] * (1.0 - drift_x[c]))))
            west.append(jnp.where(no_west, 0.0, sea[c] * (diffusion[c] * (1.0 + drift_x[c]))))
            up = sea[c] * (diffusion[c] * (1.0 - drift_y[c]))
            down = sea[c] * (diffusion[c] * (1.0 + drift_y[c]))
            if c == len(sea) - 1:
                up = jnp.where(lanes == LANES - 1, 0.0, up)
            if c == 0:
                down = jnp.where(lanes == 0, 0.0, down)
            north.append(up)
            south.append(down)
        sets = (
            (center, 0), (east, 0), (west, 0), (north, 0), (south, 0),
            (west, 1), (east, -1), (after(south), 0), (before(north), 0),
        )
        for g, (values, move) in enumerate(sets):
            for r in range(ext):
                if not 0 <= r + move < ext:
                    continue
                line = jnp.concatenate([v[r + move : r + move + 1] for v in values], axis=1)
                wide[g * ext + r] = jnp.broadcast_to(line, (SUB, columns))

    def deal_edges(low, high):
        count = REACH * half
        low_rows = low[:, :half, :].reshape(count, columns)
        high_rows = high[:, :half, :].reshape(count, columns)
        twice = deal[: 2 * columns, :]
        edges[:REACH] = dealt(low_rows, twice).reshape(REACH, half, columns)
        edges[REACH:] = dealt(high_rows, twice).reshape(REACH, half, columns)

    @pl.when(step_id == 0)
    def _():
        deal_edges(low_mine, high_mine)

    @pl.when(step_id == steps // 2)
    def _():
        deal_edges(low_theirs, high_theirs)

    def one(kt, carry):
        near = pl.ds(pl.multiple_of(kt * SUB, SUB), SUB)
        edge = pl.ds(pl.multiple_of(lax.rem(step_id, steps // 2) * block + kt * SUB, SUB), SUB)
        store = pl.ds(pl.multiple_of(turn * block + kt * SUB, SUB), SUB)

        def start(i):
            if i < 0:
                return strips_of(edges[i + REACH, edge, :])
            if i >= rows:
                return strips_of(edges[i - rows + REACH, edge, :])
            return strips_of(field_ref[i, near, :])

        for target, sets in ((fore, (0, 1, 2, 3, 4)), (back, (0, 5, 6, 7, 8))):
            levels = [{} for _ in range(REACH + 1)]
            for lead in range(-REACH, rows + REACH):
                levels[0][lead] = start(lead)
                for s in range(1, REACH + 1):
                    i = lead - s
                    if -REACH + s <= i < rows + REACH - s:
                        prev = levels[s - 1]
                        gains = [wide[g * ext + i + REACH] for g in sets]
                        shifted = (
                            prev[i], prev[i + 1], prev[i - 1], after(prev[i]), before(prev[i])
                        )
                        levels[s][i] = []
                        for c in range(columns // LANES):
                            terms = [
                                gain[:, c * LANES : (c + 1) * LANES] * value[c]
                                for gain, value in zip(gains, shifted)
                            ]
                            levels[s][i].append(
                                (terms[0] + (terms[1] + terms[2])) + (terms[3] + terms[4])
                            )
                i = lead - REACH
                if 0 <= i < rows:
                    target[i, store, :] = jnp.concatenate(levels[REACH][i], axis=1)
        return carry

    lax.fori_loop(0, block // SUB, one, 0)

    @pl.when(step_id == steps - 1)
    def _():
        out_ref[...] = jnp.zeros_like(out_ref)

        def body(i, carry):
            out_ref[...] += dot3(back[i], fore[i])
            return carry

        lax.fori_loop(0, rows, body, 0)


def prop_terms(place, model, field, edges):
    rows, width, columns = field.shape
    block = 32
    steps = width // block
    ext = rows + 2 * REACH
    vmem = pl.BlockSpec(memory_space=pltpu.VMEM)
    return pl.pallas_call(
        prop_kernel,
        grid_spec=pltpu.PrefetchScalarGridSpec(
            num_scalar_prefetch=1,
            grid=(steps,),
            in_specs=[
                vmem,
                pl.BlockSpec(
                    (rows, block, columns),
                    lambda k, place: (0, lax.rem(k + place[0] * (steps // 2), steps), 0),
                ),
                vmem,
                vmem,
                vmem,
                vmem,
            ],
            out_specs=pl.BlockSpec((width, width), lambda k, place: (0, 0)),
            scratch_shapes=[
                pltpu.VMEM((3 * columns, columns), jnp.bfloat16),
                pltpu.VMEM((4, -(-ext // SUB) * SUB, columns), jnp.float32),
                pltpu.VMEM((9 * ext, SUB, columns), jnp.float32),
                pltpu.VMEM((2 * REACH, width // 2, columns), jnp.float32),
                pltpu.VMEM((rows, width, columns), jnp.float32),
                pltpu.VMEM((rows, width, columns), jnp.float32),
            ],
        ),
        out_shape=jax.ShapeDtypeStruct((width, width), jnp.float32),
        cost_estimate=pl.CostEstimate(flops=35 * 10**9, bytes_accessed=12 * 10**6, transcendentals=0),
        name="prop_terms",
    )(place, model, field, *edges)


def eye_mask(width):
    row = lax.broadcasted_iota(jnp.int32, (width, width), 0)
    col = lax.broadcasted_iota(jnp.int32, (width, width), 1)
    return row, col


def product(left, right, passes):
    if passes == 1:
        return jnp.dot(
            left.astype(jnp.bfloat16),
            right.astype(jnp.bfloat16),
            preferred_element_type=jnp.float32,
        )
    if passes == 3:
        return dot(left, right)
    return jnp.dot(
        left, right, precision=lax.Precision.HIGHEST, preferred_element_type=jnp.float32
    )


def inverses(mats):
    width = mats[0].shape[0]
    row, col = eye_mask(width)
    identity = jnp.where(row == col, 1.0, 0.0).astype(jnp.float32)
    guesses = []
    for mat in mats:
        bound = jnp.max(jnp.sum(jnp.abs(mat), axis=0, keepdims=True), axis=1, keepdims=True)
        guesses.append(identity * (1.7 / bound))

    def stage(state, passes, goal, slowest):
        def more(state):
            turn, error, last = state[0], state[1], state[2]
            going = jnp.logical_and(error > goal, turn < 100)
            return jnp.logical_and(going, jnp.logical_or(error < slowest * last, last == 0.0))

        def improve(state):
            error = jnp.float32(0.0)
            found = []
            for mat, guess in zip(mats, state[3:]):
                rest = identity - product(mat, guess, passes[0])
                found.append(guess + product(guess, rest, passes[1]))
                error = jnp.maximum(error, jnp.sum(rest * rest))
            return (state[0] + 1, error, state[1], *found)

        return lax.while_loop(more, improve, state)

    found = guesses
    turn = jnp.int32(0)
    large = jnp.float32(1e30)
    for passes, goal, slowest in (((1, 1), 2.0, 0.5), ((3, 1), 1e-3, 0.5), ((6, 3), 1e-6, 2.0)):
        state = stage((turn, large, jnp.float32(0.0), *found), passes, goal, slowest)
        turn, found = state[0], state[3:]
    return found


def pair_kernel(
    core_ref, p_own, p_other, s_own, s_other, both_ref, send_ref, left_ref, right_ref, mid_ref
):
    tiles, _, width = s_own.shape
    part = width // tiles
    first = core_ref[0] == 0
    row, col = eye_mask(width)
    identity = jnp.where(row == col, 1.0, 0.0).astype(jnp.float32)

    def ordered(own, other):
        return jnp.where(first, own, other), jnp.where(first, other, own)

    p_left, p_right = ordered(p_own[...], p_other[...])
    info = ordered(
        jnp.concatenate([s_own[t, :part, :] for t in range(tiles)], axis=0),
        jnp.concatenate([s_other[t, :part, :] for t in range(tiles)], axis=0),
    )
    rhs_left, rhs_right = ordered(s_own[0, part:, :], s_other[0, part:, :])
    square_left = dot(p_left, p_left, (0, 0))
    square_right = dot(p_right, p_right, (0, 0))
    middle = (Q + 2 * RIDGE) * identity + info[0] + Q * square_right
    (back,) = inverses([middle])
    toward_left = dot(p_left, back, (0, 0))
    toward_right = dot(jnp.concatenate([p_right, rhs_left], axis=0), back)
    mid = toward_right[width:]
    toward_right = toward_right[:width]
    by_left = dot(jnp.concatenate([toward_left, mid], axis=0), p_left)
    by_right = dot(jnp.concatenate([toward_left, toward_right, mid], axis=0), p_right, (1, 1))
    upper = Q * square_left + RIDGE * identity - (Q * Q) * by_left[:width]
    cross = -(Q * Q) * by_right[:width]
    lower = (Q + RIDGE) * identity + info[1] - (Q * Q) * by_right[width : 2 * width]
    head = Q * by_left[width:]
    tail = rhs_right + Q * by_right[2 * width :]
    lower_diag = jnp.sum(jnp.where(row == col, lower, 0.0), axis=0, keepdims=True)
    both_ref[0, :width, :] = jnp.where(row >= col, upper, lower)
    small = lax.broadcasted_iota(jnp.int32, (TAIL, width), 0)
    both_ref[0, width:, :] = jnp.where(small == 0, lower_diag, jnp.where(small == 1, head, tail))
    both_ref[1, :width, :] = cross
    both_ref[1, width:, :] = jnp.zeros((TAIL, width), jnp.float32)
    send_ref[...] = jnp.where(first, both_ref[0], both_ref[1])
    left_ref[...] = Q * toward_left
    right_ref[...] = Q * toward_right
    mid_ref[...] = mid


def merge_pair(core, *terms):
    width = terms[0].shape[1]
    vmem = pl.BlockSpec(memory_space=pltpu.VMEM)
    block = jax.ShapeDtypeStruct((width, width), jnp.float32)
    return pl.pallas_call(
        pair_kernel,
        in_specs=[pl.BlockSpec(memory_space=pltpu.SMEM)] + [vmem] * 4,
        out_specs=[vmem] * 5,
        out_shape=[
            jax.ShapeDtypeStruct((2, width + TAIL, width), jnp.float32),
            jax.ShapeDtypeStruct((width + TAIL, width), jnp.float32),
            block,
            block,
            jax.ShapeDtypeStruct((TAIL, width), jnp.float32),
        ],
        name="merge_pair",
    )(core, *terms)


def chain_kernel(
    place_ref, both_ref, m_prev, o_prev, m_next, o_next, m_far, o_far, left_ref, right_ref, mid_ref,
    basis_ref, coeff_ref, end_ref, blocks, states, basis, weight, sem,
):
    fetch = pltpu.make_async_copy(basis_ref, basis, sem)
    fetch.start()
    core, chip = place_ref[0], place_ref[1]
    width = both_ref.shape[2]
    row, col = eye_mask(width)
    blocks[chip] = both_ref[...]
    for mine, theirs, move in ((m_prev, o_prev, 3), (m_next, o_next, 1), (m_far, o_far, 2)):
        at = lax.rem(chip + move, 4)
        blocks[at, core] = mine[...]
        blocks[at, 1 - core] = theirs[...]
    upper, lower, cross, head, tail = [], [], [], [], []
    for c in range(4):
        packed = blocks[c, 0, :width, :]
        turned = packed.T
        small = blocks[c, 0, width:, :]
        upper.append(jnp.where(row >= col, packed, turned))
        off = jnp.where(row < col, packed, turned)
        lower.append(jnp.where(row == col, jnp.broadcast_to(small[0:1], (width, width)), off))
        head.append(jnp.broadcast_to(small[1:2], (TAIL, width)))
        tail.append(jnp.broadcast_to(small[2:3], (TAIL, width)))
        cross.append(blocks[c, 1, :width, :])
    diag = [upper[0], lower[0] + upper[1], lower[1] + upper[2], lower[2] + upper[3], lower[3]]
    rhs = [head[0], tail[0] + head[1], tail[1] + head[2], tail[2] + head[3], tail[3]]
    inv0, inv2, inv4 = inverses([diag[0], diag[2], diag[4]])
    t10 = dot(cross[0], inv0, (0, 0))
    t12 = dot(cross[1], inv2)
    t32 = dot(cross[2], inv2, (0, 0))
    t34 = dot(cross[3], inv4)
    z0, z2, z4 = dot(rhs[0], inv0), dot(rhs[2], inv2), dot(rhs[4], inv4)
    diag1 = diag[1] - dot(t10, cross[0]) - dot(t12, cross[1], (1, 1))
    diag3 = diag[3] - dot(t32, cross[2]) - dot(t34, cross[3], (1, 1))
    link = -dot(t12, cross[2])
    rhs1 = rhs[1] - dot(z0, cross[0]) - dot(z2, cross[1], (1, 1))
    rhs3 = rhs[3] - dot(z2, cross[2]) - dot(z4, cross[3], (1, 1))
    (inv1,) = inverses([diag1])
    t31 = dot(link, inv1, (0, 0))
    z1 = dot(rhs1, inv1)
    diag3 = diag3 - dot(t31, link)
    rhs3 = rhs3 - dot(z1, link)
    (inv3,) = inverses([diag3])
    y3 = dot(rhs3, inv3)
    y1 = z1 - dot(y3, t31)
    y0 = z0 - dot(y1, t10)
    y2 = z2 - dot(y1, t12) - dot(y3, t32)
    y4 = z4 - dot(y3, t34)
    for c, state in enumerate((y0, y1, y2, y3, y4)):
        states[c] = state
    begin, finish = states[chip], states[chip + 1]
    inner = mid_ref[...] + dot(begin, left_ref[...]) + dot(finish, right_ref[...])
    first = core == 0
    start = jnp.where(first, begin, inner)
    end = jnp.where(first, inner, finish)
    coeff_ref[0, 0:1, :] = start[0:1]
    coeff_ref[0, 1:2, :] = end[0:1]
    weight[...] = jnp.concatenate([end] * (LANES // TAIL), axis=0).T
    rows, columns = end_ref.shape[1:]
    fetch.wait()

    def add(k, total):
        line = basis[pl.ds(pl.multiple_of(k * rows, rows), rows), :]
        factor = jnp.broadcast_to(weight[pl.ds(k, 1), :], (rows, LANES))
        return total + line * jnp.concatenate([factor] * (columns // LANES), axis=1)

    end_ref[0] = lax.fori_loop(0, width, add, jnp.zeros((rows, columns), jnp.float32), unroll=8)


def solve_chain(place, both, received, left, right, mid, basis2, rows):
    width = both.shape[2]
    columns = basis2.shape[1]
    vmem = pl.BlockSpec(memory_space=pltpu.VMEM)
    return pl.pallas_call(
        chain_kernel,
        in_specs=[pl.BlockSpec(memory_space=pltpu.SMEM)]
        + [vmem] * 10
        + [pl.BlockSpec(memory_space=pltpu.HBM)],
        out_specs=[vmem, vmem],
        out_shape=[
            jax.ShapeDtypeStruct((1, 2, width), jnp.float32),
            jax.ShapeDtypeStruct((1, rows, columns), jnp.float32),
        ],
        scratch_shapes=[
            pltpu.VMEM((4, 2, width + TAIL, width), jnp.float32),
            pltpu.VMEM((5, TAIL, width), jnp.float32),
            pltpu.VMEM(basis2.shape, jnp.float32),
            pltpu.VMEM((width, LANES), jnp.float32),
            pltpu.SemaphoreType.DMA,
        ],
        name="solve_chain",
    )(place, both, *received, left, right, mid, basis2)


def shift(value, axis, step, wrap):
    size = lax.axis_size(axis)
    pairs = [(i, (i + step) % size) for i in range(size) if wrap or 0 <= i + step < size]
    return lax.ppermute(value, axis, pairs)


def swap_core(value):
    return lax.ppermute(value, "tm", [(i, i ^ 1) for i in range(lax.axis_size("tm"))])


def tile_sum(pieces, scale):
    slices = lax.all_to_all(pieces, "tile", 0, 0, tiled=True)
    mine = jnp.sum(slices, axis=0) * scale
    return lax.all_to_all(jnp.broadcast_to(mine[None], pieces.shape), "tile", 0, 0, tiled=True)


def obs_maps(cells, values, rows, columns):
    local = cells - lax.axis_index("tile") * (rows * columns)
    row = local // columns
    col = local & (columns - 1)
    strips = columns // LANES
    col = (col % strips) * LANES + col // strips
    by_row = (row[None, :] == jnp.arange(rows)[:, None]).astype(jnp.float32)
    by_col = (col[:, None] == jnp.arange(columns)[None, :]).astype(jnp.float32)
    both = jnp.concatenate([by_row, by_row * values[None, :]], axis=0)
    maps = jnp.dot(both, by_col, precision=lax.Precision.HIGHEST)
    return maps[:rows], maps[rows:]


def shards(basis, diffusion, drift_x, drift_y, land_sea, obs_cells, obs_values):
    width, rows, columns = basis.shape
    tiles = lax.axis_size("tile")
    group = lax.axis_index("tm")
    core = group & 1
    chip = group >> 1
    basis2 = basis.reshape(width * rows, columns)
    models = (diffusion, drift_x, drift_y, land_sea[None])
    low_send, high_send, model = edge_terms(core[None], models, basis2, width, rows)
    low = shift(low_send, "tile", 1, False)
    high = shift(high_send, "tile", -1, False)
    edges = (low, swap_core(low), high, swap_core(high))
    count, value = obs_maps(obs_cells[0], obs_values[0], rows, columns)
    field, obs = lay_basis(basis2, count, value, width, rows, tiles)
    place = jnp.stack([core, lax.axis_index("tile"), jnp.int32(tiles - 1)])
    s_own = tile_sum(obs, 1.0 / float(NOBS))
    s_other = swap_core(s_own)
    prop = prop_terms(place, model, field, edges)
    cells = float(tiles * rows * columns)
    p_own = tile_sum(prop.reshape(tiles, width // tiles, width), 1.0 / cells).reshape(width, width)
    p_other = swap_core(p_own)

    both, send, left, right, mid = merge_pair(core[None], p_own, p_other, s_own, s_other)
    prev_mine = shift(send, "tm", 2, True)
    next_mine = shift(send, "tm", -2, True)
    size = lax.axis_size("tm")
    onward = [(i, (i + (2 if i % 2 == 0 else size - 2)) % size) for i in range(size)]
    far_mine = lax.ppermute(jnp.where(core == 0, prev_mine, next_mine), "tm", onward)
    received = []
    for mine in (prev_mine, next_mine, far_mine):
        received += [mine, swap_core(mine)]
    place = jnp.stack([core, chip])
    return tuple(solve_chain(place, both, received, left, right, mid, basis2, rows))


def solution(mesh):
    in_specs = (
        P(None, "tile", None),
        P("tm", "tile", None),
        P("tm", "tile", None),
        P("tm", "tile", None),
        P("tile", None),
        P("tm", None),
        P("tm", None),
    )
    out_specs = (P("tm", None, None), P("tm", "tile", None))
    return jax.shard_map(shards, mesh=mesh, in_specs=in_specs, out_specs=out_specs, check_vma=False)
```

```python
import functools

import jax
import jax.numpy as jnp
from jax import lax
from jax.experimental import pallas as pl
from jax.experimental.pallas import tpu as pltpu
from jax.sharding import PartitionSpec as P

STEPS = 6
REACH = STEPS // 2
NOBS = 512
Q = 10.0
RIDGE = 0.1
SUB = 8
LANES = 128
TAIL = 8
CHIPS = 4


def split(value):
    high = value.astype(jnp.bfloat16)
    low = (value - high.astype(jnp.float32)).astype(jnp.bfloat16)
    return high, low


def dot3(left, right):
    lh, ll = split(left)
    rh, rl = split(right)
    return lax.dot_general(
        jnp.concatenate([lh, lh, ll], axis=1),
        jnp.concatenate([rh, rl, rh], axis=1),
        (((1,), (1,)), ((), ())),
        preferred_element_type=jnp.float32,
    )


def dot(left, right, contract=(1, 0)):
    lh, ll = split(left)
    rh, rl = split(right)
    return lax.dot_general(
        jnp.concatenate([lh, lh, ll], axis=contract[0]),
        jnp.concatenate([rh, rl, rh], axis=contract[1]),
        (((contract[0],), (contract[1],)), ((), ())),
        preferred_element_type=jnp.float32,
    )


def deal_matrix(columns, copies):
    strips = columns // LANES
    source = lax.broadcasted_iota(jnp.int32, (columns, columns), 0)
    target = lax.broadcasted_iota(jnp.int32, (columns, columns), 1)
    wanted = (target % LANES) * strips + target // LANES
    one = jnp.where(source == wanted, 1.0, 0.0).astype(jnp.bfloat16)
    return jnp.concatenate([one] * copies, axis=0)


def dealt(value, deal):
    parts, rest = [], value
    for _ in range(deal.shape[0] // deal.shape[1]):
        part = rest.astype(jnp.bfloat16)
        parts.append(part)
        rest = rest - part.astype(jnp.float32)
    return jnp.dot(jnp.concatenate(parts, axis=1), deal, preferred_element_type=jnp.float32)


def strips_of(value):
    return [value[:, c : c + LANES] for c in range(0, value.shape[1], LANES)]


def after(strips):
    return strips[1:] + [pltpu.roll(strips[0], LANES - 1, 1)]


def before(strips):
    return [pltpu.roll(strips[-1], 1, 1)] + strips[:-1]


def edge_kernel(rows, core_ref, *refs):
    model_refs, basis_refs, (low_ref, high_ref, model_ref) = refs[:4], refs[4:-3], refs[-3:]
    step_id = pl.program_id(0)
    block = basis_refs[0].shape[0] // rows
    half = low_ref.shape[1] - TAIL

    @pl.when(step_id == 0)
    def _():
        for f, ref in enumerate(model_refs):
            model_ref[f] = ref[0].astype(jnp.float32)
        for r in range(REACH):
            low_ref[r, half:, :] = jnp.zeros_like(low_ref[r, half:, :])
            high_ref[r, half:, :] = jnp.zeros_like(high_ref[r, half:, :])
            for f in range(4):
                at = rows - REACH + r
                low_ref[r, half + f : half + f + 1, :] = model_ref[f, at : at + 1, :]
                high_ref[r, half + f : half + f + 1, :] = model_ref[f, r : r + 1, :]

    store = pl.ds(pl.multiple_of(step_id * block, block), block)
    for r in range(REACH):
        for out, i in ((low_ref, rows - REACH + r), (high_ref, r)):
            span = pl.ds(i, block, stride=rows)
            out[r, store, :] = jnp.concatenate([ref[span, :] for ref in basis_refs], axis=1)


def edge_terms(core, models, basis2, width, rows):
    columns = basis2.shape[1]
    block = 32
    strips = columns // LANES
    steps = width // 2 // block
    own = pl.BlockSpec((1, rows, columns), lambda k, core: (0, 0, 0))
    edge = (REACH, width // 2 + TAIL, columns)
    return pl.pallas_call(
        functools.partial(edge_kernel, rows),
        grid_spec=pltpu.PrefetchScalarGridSpec(
            num_scalar_prefetch=1,
            grid=(steps,),
            in_specs=[own] * 4
            + [
                pl.BlockSpec((block * rows, LANES), lambda k, core, c=c: (k + core[0] * steps, c))
                for c in range(strips)
            ],
            out_specs=[
                pl.BlockSpec(edge, lambda k, core: (0, 0, 0)),
                pl.BlockSpec(edge, lambda k, core: (0, 0, 0)),
                pl.BlockSpec((4, rows, columns), lambda k, core: (0, 0, 0)),
            ],
        ),
        out_shape=[
            jax.ShapeDtypeStruct(edge, jnp.float32),
            jax.ShapeDtypeStruct(edge, jnp.float32),
            jax.ShapeDtypeStruct((4, rows, columns), jnp.float32),
        ],
        name="edge_terms",
    )(core, *models, *[basis2] * strips)


def lay_kernel(rows, count_ref, value_ref, *refs):
    basis_refs, (field_ref, out_ref, deal, held) = refs[:-4], refs[-4:]
    step_id = pl.program_id(0)
    width = held.shape[1]
    block = basis_refs[0].shape[0] // rows

    @pl.when(step_id == 0)
    def _():
        deal[...] = deal_matrix(deal.shape[1], 2)

    lines = []
    for i in range(rows):
        span = pl.ds(i, block, stride=rows)
        lines.append(jnp.concatenate([ref[span, :] for ref in basis_refs], axis=1))
    laid = dealt(jnp.concatenate(lines, axis=0), deal[...])
    at = pl.ds(pl.multiple_of(step_id * block, block), block)
    for i in range(rows):
        line = laid[i * block : (i + 1) * block]
        field_ref[i] = line
        held[i, at, :] = line

    @pl.when(step_id == pl.num_programs(0) - 1)
    def _():
        out_ref[...] = jnp.zeros_like(out_ref)
        tiles = out_ref.shape[0]
        part = width // tiles

        def body(i, carry):
            field = held[i]
            count = count_ref[pl.ds(i, 1), :]
            value = jnp.broadcast_to(value_ref[pl.ds(i, 1), :], (TAIL, count.shape[1]))
            terms = dot3(jnp.concatenate([field * count, value], axis=0), field)
            for t in range(tiles):
                out_ref[t, :part, :] += terms[t * part : (t + 1) * part]
            out_ref[0, part:, :] += terms[width:]
            return carry

        lax.fori_loop(0, rows, body, 0)


def lay_basis(basis2, count, value, width, rows, tiles):
    columns = basis2.shape[1]
    block = 32
    strips = columns // LANES
    return pl.pallas_call(
        functools.partial(lay_kernel, rows),
        grid=(width // block,),
        in_specs=[
            pl.BlockSpec((rows, columns), lambda k: (0, 0)),
            pl.BlockSpec((rows, columns), lambda k: (0, 0)),
            *[pl.BlockSpec((block * rows, LANES), lambda k, c=c: (k, c)) for c in range(strips)],
        ],
        out_specs=[
            pl.BlockSpec((rows, block, columns), lambda k: (0, k, 0)),
            pl.BlockSpec((tiles, width // tiles + TAIL, width), lambda k: (0, 0, 0)),
        ],
        out_shape=[
            jax.ShapeDtypeStruct((rows, width, columns), jnp.float32),
            jax.ShapeDtypeStruct((tiles, width // tiles + TAIL, width), jnp.float32),
        ],
        scratch_shapes=[
            pltpu.VMEM((2 * columns, columns), jnp.bfloat16),
            pltpu.VMEM((rows, width, columns), jnp.float32),
        ],
        cost_estimate=pl.CostEstimate(flops=20 * 10**9, bytes_accessed=17 * 10**6, transcendentals=0),
        name="lay_basis",
    )(count, value, *[basis2] * strips)


def prop_kernel(
    place_ref, model_ref, field_ref, low_mine, low_theirs, high_mine, high_theirs, obs_ref,
    out_ref, deal, model, wide, edges, fore, back,
):
    step_id = pl.program_id(0)
    steps = pl.num_programs(0)
    rows, block, columns = field_ref.shape
    ext = rows + 2 * REACH
    width = fore.shape[1]
    half = width // 2
    core, tile, last_tile = place_ref[0], place_ref[1], place_ref[2]
    turn = lax.rem(step_id + core * (steps // 2), steps)

    @pl.when(step_id == 0)
    def _():
        deal[...] = deal_matrix(columns, 3)
        model[...] = jnp.zeros_like(model)
        for f in range(4):
            for r in range(REACH):
                model[f, r : r + 1, :] = low_mine[r, half + f : half + f + 1, :]
                at = REACH + rows + r
                model[f, at : at + 1, :] = high_mine[r, half + f : half + f + 1, :]
            for r in range(rows):
                model[f, REACH + r : REACH + r + 1, :] = model_ref[f, r : r + 1, :]
        tall = model.shape[1]
        together = dealt(model[...].reshape(4 * tall, columns), deal[...])
        lines = lax.broadcasted_iota(jnp.int32, (tall, LANES), 0)
        lanes = lax.broadcasted_iota(jnp.int32, (tall, LANES), 1)
        no_west = jnp.logical_and(tile == 0, lines == REACH)
        no_east = jnp.logical_and(tile == last_tile, lines == REACH + rows - 1)
        diffusion, drift_x, drift_y, sea = (
            strips_of(together[f * tall : (f + 1) * tall]) for f in range(4)
        )
        center, east, west, north, south = [], [], [], [], []
        for c in range(len(sea)):
            center.append(sea[c] * (1.0 - 4.0 * diffusion[c]))
            east.append(jnp.where(no_east, 0.0, sea[c] * (diffusion[c] * (1.0 - drift_x[c]))))
            west.append(jnp.where(no_west, 0.0, sea[c] * (diffusion[c] * (1.0 + drift_x[c]))))
            up = sea[c] * (diffusion[c] * (1.0 - drift_y[c]))
            down = sea[c] * (diffusion[c] * (1.0 + drift_y[c]))
            if c == len(sea) - 1:
                up = jnp.where(lanes == LANES - 1, 0.0, up)
            if c == 0:
                down = jnp.where(lanes == 0, 0.0, down)
            north.append(up)
            south.append(down)
        sets = (
            (center, 0), (east, 0), (west, 0), (north, 0), (south, 0),
            (west, 1), (east, -1), (after(south), 0), (before(north), 0),
        )
        for g, (values, move) in enumerate(sets):
            for r in range(ext):
                if not 0 <= r + move < ext:
                    continue
                line = jnp.concatenate([v[r + move : r + move + 1] for v in values], axis=1)
                wide[g * ext + r] = jnp.broadcast_to(line, (SUB, columns))

    def deal_edges(low, high):
        count = REACH * half
        low_rows = low[:, :half, :].reshape(count, columns)
        high_rows = high[:, :half, :].reshape(count, columns)
        twice = deal[: 2 * columns, :]
        edges[:REACH] = dealt(low_rows, twice).reshape(REACH, half, columns)
        edges[REACH:] = dealt(high_rows, twice).reshape(REACH, half, columns)

    @pl.when(step_id == 0)
    def _():
        deal_edges(low_mine, high_mine)

    @pl.when(step_id == steps // 2)
    def _():
        deal_edges(low_theirs, high_theirs)

    def one(kt, carry):
        near = pl.ds(pl.multiple_of(kt * SUB, SUB), SUB)
        edge = pl.ds(pl.multiple_of(lax.rem(step_id, steps // 2) * block + kt * SUB, SUB), SUB)
        store = pl.ds(pl.multiple_of(turn * block + kt * SUB, SUB), SUB)

        def start(i):
            if i < 0:
                return strips_of(edges[i + REACH, edge, :])
            if i >= rows:
                return strips_of(edges[i - rows + REACH, edge, :])
            return strips_of(field_ref[i, near, :])

        for target, sets in ((fore, (0, 1, 2, 3, 4)), (back, (0, 5, 6, 7, 8))):
            levels = [{} for _ in range(REACH + 1)]
            for lead in range(-REACH, rows + REACH):
                levels[0][lead] = start(lead)
                for s in range(1, REACH + 1):
                    i = lead - s
                    if -REACH + s <= i < rows + REACH - s:
                        prev = levels[s - 1]
                        gains = [wide[g * ext + i + REACH] for g in sets]
                        shifted = (
                            prev[i], prev[i + 1], prev[i - 1], after(prev[i]), before(prev[i])
                        )
                        levels[s][i] = []
                        for c in range(columns // LANES):
                            terms = [
                                gain[:, c * LANES : (c + 1) * LANES] * value[c]
                                for gain, value in zip(gains, shifted)
                            ]
                            levels[s][i].append(
                                (terms[0] + (terms[1] + terms[2])) + (terms[3] + terms[4])
                            )
                i = lead - REACH
                if 0 <= i < rows:
                    target[i, store, :] = jnp.concatenate(levels[REACH][i], axis=1)
        return carry

    lax.fori_loop(0, block // SUB, one, 0)

    @pl.when(step_id == steps - 1)
    def _():
        tiles = out_ref.shape[0]
        part = width // tiles
        out_ref[:, :part, :] = jnp.zeros_like(out_ref[:, :part, :])
        out_ref[:, part:, :] = obs_ref[...]

        def body(i, carry):
            terms = dot3(back[i], fore[i])
            for t in range(tiles):
                out_ref[t, :part, :] += terms[t * part : (t + 1) * part]
            return carry

        lax.fori_loop(0, rows, body, 0)


def prop_terms(place, model, field, edges, obs):
    rows, width, columns = field.shape
    block = 32
    steps = width // block
    ext = rows + 2 * REACH
    vmem = pl.BlockSpec(memory_space=pltpu.VMEM)
    tiles, lines, _ = obs.shape
    total = (tiles, width // tiles + lines, width)
    return pl.pallas_call(
        prop_kernel,
        grid_spec=pltpu.PrefetchScalarGridSpec(
            num_scalar_prefetch=1,
            grid=(steps,),
            in_specs=[
                vmem,
                pl.BlockSpec(
                    (rows, block, columns),
                    lambda k, place: (0, lax.rem(k + place[0] * (steps // 2), steps), 0),
                ),
                vmem,
                vmem,
                vmem,
                vmem,
                vmem,
            ],
            out_specs=pl.BlockSpec(total, lambda k, place: (0, 0, 0)),
            scratch_shapes=[
                pltpu.VMEM((3 * columns, columns), jnp.bfloat16),
                pltpu.VMEM((4, -(-ext // SUB) * SUB, columns), jnp.float32),
                pltpu.VMEM((9 * ext, SUB, columns), jnp.float32),
                pltpu.VMEM((2 * REACH, width // 2, columns), jnp.float32),
                pltpu.VMEM((rows, width, columns), jnp.float32),
                pltpu.VMEM((rows, width, columns), jnp.float32),
            ],
        ),
        out_shape=jax.ShapeDtypeStruct(total, jnp.float32),
        cost_estimate=pl.CostEstimate(flops=35 * 10**9, bytes_accessed=12 * 10**6, transcendentals=0),
        name="prop_terms",
    )(place, model, field, *edges, obs)


def eye_mask(width):
    row = lax.broadcasted_iota(jnp.int32, (width, width), 0)
    col = lax.broadcasted_iota(jnp.int32, (width, width), 1)
    return row, col


def product(left, right, passes):
    if passes == 1:
        return jnp.dot(
            left.astype(jnp.bfloat16),
            right.astype(jnp.bfloat16),
            preferred_element_type=jnp.float32,
        )
    if passes == 3:
        return dot(left, right)
    return jnp.dot(
        left, right, precision=lax.Precision.HIGHEST, preferred_element_type=jnp.float32
    )


def inverses(mats):
    width = mats[0].shape[0]
    row, col = eye_mask(width)
    identity = jnp.where(row == col, 1.0, 0.0).astype(jnp.float32)
    guesses = []
    for mat in mats:
        bound = jnp.max(jnp.sum(jnp.abs(mat), axis=0, keepdims=True), axis=1, keepdims=True)
        trace = jnp.sum(jnp.sum(identity * mat, axis=0, keepdims=True), axis=1, keepdims=True)
        square = jnp.sum(jnp.sum(mat * mat, axis=0, keepdims=True), axis=1, keepdims=True)
        guesses.append(identity * jnp.minimum(trace / square, 1.9 / bound))

    def stage(state, passes, goal, slowest):
        def more(state):
            turn, error, last = state[0], state[1], state[2]
            going = jnp.logical_and(error > goal, turn < 100)
            return jnp.logical_and(going, jnp.logical_or(error < slowest * last, last == 0.0))

        def improve(state):
            error = jnp.float32(0.0)
            found = []
            for mat, guess in zip(mats, state[3:]):
                rest = identity - product(mat, guess, passes[0])
                found.append(guess + product(guess, rest, passes[1]))
                error = jnp.maximum(error, jnp.sum(rest * rest))
            return (state[0] + 1, error, state[1], *found)

        return lax.while_loop(more, improve, state)

    found = guesses
    turn = jnp.int32(0)
    large = jnp.float32(1e30)
    for passes, goal, slowest in (((1, 1), 2.0, 0.5), ((3, 1), 1e-3, 0.5), ((6, 3), 1e-6, 2.0)):
        state = stage((turn, large, jnp.float32(0.0), *found), passes, goal, slowest)
        turn, found = state[0], state[3:]
    return found


def pair_kernel(
    place_ref, own_ref, other_ref, both_ref, send_ref, left_ref, right_ref, outer_ref, small_ref
):
    tiles, _, width = own_ref.shape
    part = width // tiles
    core, chip = place_ref[0], place_ref[1]
    first = core == 0
    row, col = eye_mask(width)
    identity = jnp.where(row == col, 1.0, 0.0).astype(jnp.float32)

    def ordered(own, other):
        return jnp.where(first, own, other), jnp.where(first, other, own)

    def stacked(ref, at):
        return jnp.concatenate([ref[t, at : at + part, :] for t in range(tiles)], axis=0)

    p_left, p_right = ordered(stacked(own_ref, 0), stacked(other_ref, 0))
    info = ordered(stacked(own_ref, part), stacked(other_ref, part))
    rhs_left, rhs_right = ordered(own_ref[0, 2 * part :, :], other_ref[0, 2 * part :, :])
    square_left = dot(p_left, p_left, (0, 0))
    square_right = dot(p_right, p_right, (0, 0))
    middle = (Q + 2 * RIDGE) * identity + info[0] + Q * square_right
    (back,) = inverses([middle])
    toward_left = dot(p_left, back, (0, 0))
    toward_right = dot(jnp.concatenate([p_right, rhs_left], axis=0), back)
    mid = toward_right[width:]
    toward_right = toward_right[:width]
    by_left = dot(jnp.concatenate([toward_left, mid], axis=0), p_left)
    by_right = dot(jnp.concatenate([toward_left, toward_right, mid], axis=0), p_right, (1, 1))
    upper = Q * square_left + RIDGE * identity - (Q * Q) * by_left[:width]
    cross = -(Q * Q) * by_right[:width]
    lower = (Q + RIDGE) * identity + info[1] - (Q * Q) * by_right[width : 2 * width]
    head = Q * by_left[width:]
    tail = rhs_right + Q * by_right[2 * width :]
    both_ref[1, :width, :] = cross
    left_ref[...] = Q * toward_left
    right_ref[...] = Q * toward_right
    outer_ref[...] = jnp.zeros_like(outer_ref)
    small_ref[...] = jnp.zeros_like(small_ref)
    small_ref[0] = mid
    lines = lax.broadcasted_iota(jnp.int32, (TAIL, width), 0)

    def pack(upper, lower, head, tail):
        lower_diag = jnp.sum(jnp.where(row == col, lower, 0.0), axis=0, keepdims=True)
        both_ref[0, :width, :] = jnp.where(row >= col, upper, lower)
        both_ref[0, width:, :] = jnp.where(lines == 0, lower_diag, jnp.where(lines == 1, head, tail))

    opening, closing = chip == 0, chip == CHIPS - 1
    outer = jnp.logical_or(opening, closing)

    @pl.when(outer)
    def _():
        gone = jnp.where(opening, upper, lower)
        kept = jnp.where(opening, lower, upper)
        joint = jnp.where(opening, cross, cross.T)
        gone_rhs = jnp.where(opening, head, tail)
        kept_rhs = jnp.where(opening, tail, head)
        (gone_back,) = inverses([gone])
        toward = dot(joint, gone_back, (0, 0))
        rest = dot(gone_rhs, gone_back)
        both = dot(jnp.concatenate([toward, rest], axis=0), joint)
        kept = kept - both[:width]
        kept_rhs = kept_rhs - both[width:]
        outer_ref[...] = toward
        small_ref[1] = rest
        pack(kept, kept, kept_rhs, kept_rhs)

    @pl.when(jnp.logical_not(outer))
    def _():
        pack(upper, lower, head, tail)

    both_ref[1, width:, :] = jnp.zeros((TAIL, width), jnp.float32)
    send_ref[...] = jnp.where(first, both_ref[0], both_ref[1])


def merge_pair(place, own, other):
    width = own.shape[2]
    vmem = pl.BlockSpec(memory_space=pltpu.VMEM)
    block = jax.ShapeDtypeStruct((width, width), jnp.float32)
    return pl.pallas_call(
        pair_kernel,
        in_specs=[pl.BlockSpec(memory_space=pltpu.SMEM)] + [vmem] * 2,
        out_specs=[vmem] * 6,
        out_shape=[
            jax.ShapeDtypeStruct((2, width + TAIL, width), jnp.float32),
            jax.ShapeDtypeStruct((width + TAIL, width), jnp.float32),
            block,
            block,
            block,
            jax.ShapeDtypeStruct((2, TAIL, width), jnp.float32),
        ],
        name="merge_pair",
    )(place, own, other)


def chain_kernel(
    place_ref, both_ref, m_prev, o_prev, m_next, o_next, m_far, o_far,
    left_ref, right_ref, outer_ref, small_ref,
    basis_ref, coeff_ref, end_ref, blocks, basis, weight, sem,
):
    fetch = pltpu.make_async_copy(basis_ref, basis, sem)
    fetch.start()
    core, chip = place_ref[0], place_ref[1]
    width = both_ref.shape[2]
    row, col = eye_mask(width)
    blocks[chip] = both_ref[...]
    for mine, theirs, move in ((m_prev, o_prev, 3), (m_next, o_next, 1), (m_far, o_far, 2)):
        at = lax.rem(chip + move, CHIPS)
        blocks[at, core] = mine[...]
        blocks[at, 1 - core] = theirs[...]
    upper, lower, head, tail = [], [], [], []
    for c in range(CHIPS):
        packed = blocks[c, 0, :width, :]
        turned = packed.T
        small = blocks[c, 0, width:, :]
        upper.append(jnp.where(row >= col, packed, turned))
        off = jnp.where(row < col, packed, turned)
        lower.append(jnp.where(row == col, jnp.broadcast_to(small[0:1], (width, width)), off))
        head.append(jnp.broadcast_to(small[1:2], (TAIL, width)))
        tail.append(jnp.broadcast_to(small[2:3], (TAIL, width)))
    cross1, cross2 = blocks[1, 1, :width, :], blocks[2, 1, :width, :]
    rhs1, rhs2, rhs3 = (tail[c] + head[c + 1] for c in range(3))
    inv1, inv3 = inverses([lower[0] + upper[1], lower[2] + upper[3]])
    toward1 = dot(cross1, inv1, (0, 0))
    toward3 = dot(cross2, inv3)
    z1, z3 = dot(rhs1, inv1), dot(rhs3, inv3)
    by1 = dot(jnp.concatenate([toward1, z1], axis=0), cross1)
    by3 = dot(jnp.concatenate([toward3, z3], axis=0), cross2, (1, 1))
    (inv2,) = inverses([lower[1] + upper[2] - by1[:width] - by3[:width]])
    y2 = dot(rhs2 - by1[width:] - by3[width:], inv2)
    y1 = z1 - dot(y2, toward1)
    y3 = z3 - dot(y2, toward3)
    opening = chip == 0
    y_outer = small_ref[1] - dot(jnp.where(opening, y1, y3), outer_ref[...])
    begin = jnp.where(
        opening, y_outer, jnp.where(chip == 1, y1, jnp.where(chip == 2, y2, y3))
    )
    finish = jnp.where(
        opening, y1, jnp.where(chip == 1, y2, jnp.where(chip == 2, y3, y_outer))
    )
    inner = small_ref[0] + dot(begin, left_ref[...]) + dot(finish, right_ref[...])
    first = core == 0
    start = jnp.where(first, begin, inner)
    end = jnp.where(first, inner, finish)
    coeff_ref[0, 0:1, :] = start[0:1]
    coeff_ref[0, 1:2, :] = end[0:1]
    weight[...] = jnp.concatenate([end] * (LANES // TAIL), axis=0).T
    rows, columns = end_ref.shape[1:]
    fetch.wait()

    def add(k, total):
        line = basis[pl.ds(pl.multiple_of(k * rows, rows), rows), :]
        factor = jnp.broadcast_to(weight[pl.ds(k, 1), :], (rows, LANES))
        return total + line * jnp.concatenate([factor] * (columns // LANES), axis=1)

    end_ref[0] = lax.fori_loop(0, width, add, jnp.zeros((rows, columns), jnp.float32), unroll=8)


def solve_chain(place, both, received, kept, basis2, rows):
    width = both.shape[2]
    columns = basis2.shape[1]
    vmem = pl.BlockSpec(memory_space=pltpu.VMEM)
    return pl.pallas_call(
        chain_kernel,
        in_specs=[pl.BlockSpec(memory_space=pltpu.SMEM)]
        + [vmem] * 11
        + [pl.BlockSpec(memory_space=pltpu.HBM)],
        out_specs=[vmem, vmem],
        out_shape=[
            jax.ShapeDtypeStruct((1, 2, width), jnp.float32),
            jax.ShapeDtypeStruct((1, rows, columns), jnp.float32),
        ],
        scratch_shapes=[
            pltpu.VMEM((CHIPS, 2, width + TAIL, width), jnp.float32),
            pltpu.VMEM(basis2.shape, jnp.float32),
            pltpu.VMEM((width, LANES), jnp.float32),
            pltpu.SemaphoreType.DMA,
        ],
        name="solve_chain",
    )(place, both, *received, *kept, basis2)


def shift(value, axis, step, wrap):
    size = lax.axis_size(axis)
    pairs = [(i, (i + step) % size) for i in range(size) if wrap or 0 <= i + step < size]
    return lax.ppermute(value, axis, pairs)


def swap_core(value):
    return lax.ppermute(value, "tm", [(i, i ^ 1) for i in range(lax.axis_size("tm"))])


def obs_maps(cells, values, rows, columns):
    local = cells - lax.axis_index("tile") * (rows * columns)
    row = local // columns
    col = local & (columns - 1)
    strips = columns // LANES
    col = (col % strips) * LANES + col // strips
    by_row = (row[None, :] == jnp.arange(rows)[:, None]).astype(jnp.float32)
    by_col = (col[:, None] == jnp.arange(columns)[None, :]).astype(jnp.float32)
    both = jnp.concatenate([by_row, by_row * values[None, :]], axis=0)
    maps = jnp.dot(both, by_col, precision=lax.Precision.HIGHEST)
    return maps[:rows], maps[rows:]


def shards(basis, diffusion, drift_x, drift_y, land_sea, obs_cells, obs_values):
    width, rows, columns = basis.shape
    tiles = lax.axis_size("tile")
    group = lax.axis_index("tm")
    core = group & 1
    chip = group >> 1
    basis2 = basis.reshape(width * rows, columns)
    models = (diffusion, drift_x, drift_y, land_sea[None])
    low_send, high_send, model = edge_terms(core[None], models, basis2, width, rows)
    low = shift(low_send, "tile", 1, False)
    high = shift(high_send, "tile", -1, False)
    count, value = obs_maps(obs_cells[0], obs_values[0], rows, columns)
    field, obs = lay_basis(basis2, count, value, width, rows, tiles)
    low, high, obs = lax.optimization_barrier((low, high, obs))
    edges = (low, swap_core(low), high, swap_core(high))
    place = jnp.stack([core, lax.axis_index("tile"), jnp.int32(tiles - 1)])
    terms = prop_terms(place, model, field, edges, obs)

    slices = jnp.sum(lax.all_to_all(terms, "tile", 0, 0, tiled=True), axis=0)
    lines = lax.broadcasted_iota(jnp.int32, slices.shape, 0)
    cells = float(tiles * rows * columns)
    slices = slices * jnp.where(lines < width // tiles, 1.0 / cells, 1.0 / float(NOBS))
    own = lax.all_to_all(jnp.broadcast_to(slices[None], terms.shape), "tile", 0, 0, tiled=True)
    other = swap_core(own)

    place = jnp.stack([core, chip])
    both, send, *kept = merge_pair(place, own, other)
    received = []
    for step in (2, -2, 4):
        mine = shift(send, "tm", step, True)
        received += [mine, swap_core(mine)]
    return tuple(solve_chain(place, both, received, kept, basis2, rows))


def solution(mesh):
    in_specs = (
        P(None, "tile", None),
        P("tm", "tile", None),
        P("tm", "tile", None),
        P("tm", "tile", None),
        P("tile", None),
        P("tm", None),
        P("tm", None),
    )
    out_specs = (P("tm", None, None), P("tm", "tile", None))
    return jax.shard_map(shards, mesh=mesh, in_specs=in_specs, out_specs=out_specs, check_vma=False)
```

```python
import functools

import jax
import jax.numpy as jnp
from jax import lax
from jax.experimental import pallas as pl
from jax.experimental.pallas import tpu as pltpu
from jax.sharding import PartitionSpec as P

STEPS = 6
REACH = STEPS // 2
NOBS = 512
Q = 10.0
RIDGE = 0.1
SUB = 8
LANES = 128
TAIL = 8
CHIPS = 4


def split(value):
    high = value.astype(jnp.bfloat16)
    low = (value - high.astype(jnp.float32)).astype(jnp.bfloat16)
    return high, low


def dot3(left, right):
    lh, ll = split(left)
    rh, rl = split(right)
    return lax.dot_general(
        jnp.concatenate([lh, lh, ll], axis=1),
        jnp.concatenate([rh, rl, rh], axis=1),
        (((1,), (1,)), ((), ())),
        preferred_element_type=jnp.float32,
    )


def dot(left, right, contract=(1, 0)):
    lh, ll = split(left)
    rh, rl = split(right)
    return lax.dot_general(
        jnp.concatenate([lh, lh, ll], axis=contract[0]),
        jnp.concatenate([rh, rl, rh], axis=contract[1]),
        (((contract[0],), (contract[1],)), ((), ())),
        preferred_element_type=jnp.float32,
    )


def deal_matrix(columns, copies):
    strips = columns // LANES
    source = lax.broadcasted_iota(jnp.int32, (columns, columns), 0)
    target = lax.broadcasted_iota(jnp.int32, (columns, columns), 1)
    wanted = (target % LANES) * strips + target // LANES
    one = jnp.where(source == wanted, 1.0, 0.0).astype(jnp.bfloat16)
    return jnp.concatenate([one] * copies, axis=0)


def dealt(value, deal):
    parts, rest = [], value
    for _ in range(deal.shape[0] // deal.shape[1]):
        part = rest.astype(jnp.bfloat16)
        parts.append(part)
        rest = rest - part.astype(jnp.float32)
    return jnp.dot(jnp.concatenate(parts, axis=1), deal, preferred_element_type=jnp.float32)


def strips_of(value):
    return [value[:, c : c + LANES] for c in range(0, value.shape[1], LANES)]


def after(strips):
    return strips[1:] + [pltpu.roll(strips[0], LANES - 1, 1)]


def before(strips):
    return [pltpu.roll(strips[-1], 1, 1)] + strips[:-1]


def edge_kernel(rows, core_ref, *refs):
    model_refs, basis_refs, (low_ref, high_ref, model_ref) = refs[:4], refs[4:-3], refs[-3:]
    step_id = pl.program_id(0)
    block = basis_refs[0].shape[0] // rows
    half = low_ref.shape[1] - TAIL

    @pl.when(step_id == 0)
    def _():
        for f, ref in enumerate(model_refs):
            model_ref[f] = ref[0].astype(jnp.float32)
        for r in range(REACH):
            low_ref[r, half:, :] = jnp.zeros_like(low_ref[r, half:, :])
            high_ref[r, half:, :] = jnp.zeros_like(high_ref[r, half:, :])
            for f in range(4):
                at = rows - REACH + r
                low_ref[r, half + f : half + f + 1, :] = model_ref[f, at : at + 1, :]
                high_ref[r, half + f : half + f + 1, :] = model_ref[f, r : r + 1, :]

    store = pl.ds(pl.multiple_of(step_id * block, block), block)
    for r in range(REACH):
        for out, i in ((low_ref, rows - REACH + r), (high_ref, r)):
            span = pl.ds(i, block, stride=rows)
            out[r, store, :] = jnp.concatenate([ref[span, :] for ref in basis_refs], axis=1)


def edge_terms(core, models, basis2, width, rows):
    columns = basis2.shape[1]
    block = 32
    strips = columns // LANES
    steps = width // 2 // block
    own = pl.BlockSpec((1, rows, columns), lambda k, core: (0, 0, 0))
    edge = (REACH, width // 2 + TAIL, columns)
    return pl.pallas_call(
        functools.partial(edge_kernel, rows),
        grid_spec=pltpu.PrefetchScalarGridSpec(
            num_scalar_prefetch=1,
            grid=(steps,),
            in_specs=[own] * 4
            + [
                pl.BlockSpec((block * rows, LANES), lambda k, core, c=c: (k + core[0] * steps, c))
                for c in range(strips)
            ],
            out_specs=[
                pl.BlockSpec(edge, lambda k, core: (0, 0, 0)),
                pl.BlockSpec(edge, lambda k, core: (0, 0, 0)),
                pl.BlockSpec((4, rows, columns), lambda k, core: (0, 0, 0)),
            ],
        ),
        out_shape=[
            jax.ShapeDtypeStruct(edge, jnp.float32),
            jax.ShapeDtypeStruct(edge, jnp.float32),
            jax.ShapeDtypeStruct((4, rows, columns), jnp.float32),
        ],
        name="edge_terms",
    )(core, *models, *[basis2] * strips)


def lay_kernel(rows, count_ref, value_ref, *refs):
    basis_refs, (field_ref, out_ref, deal, held) = refs[:-4], refs[-4:]
    step_id = pl.program_id(0)
    width = held.shape[1]
    block = basis_refs[0].shape[0] // rows

    @pl.when(step_id == 0)
    def _():
        deal[...] = deal_matrix(deal.shape[1], 2)

    lines = []
    for i in range(rows):
        span = pl.ds(i, block, stride=rows)
        lines.append(jnp.concatenate([ref[span, :] for ref in basis_refs], axis=1))
    laid = dealt(jnp.concatenate(lines, axis=0), deal[...])
    at = pl.ds(pl.multiple_of(step_id * block, block), block)
    for i in range(rows):
        line = laid[i * block : (i + 1) * block]
        field_ref[i] = line
        held[i, at, :] = line

    @pl.when(step_id == pl.num_programs(0) - 1)
    def _():
        out_ref[...] = jnp.zeros_like(out_ref)
        tiles = out_ref.shape[0]
        part = width // tiles

        def body(i, carry):
            field = held[i]
            count = count_ref[pl.ds(i, 1), :]
            value = jnp.broadcast_to(value_ref[pl.ds(i, 1), :], (TAIL, count.shape[1]))
            terms = dot3(jnp.concatenate([field * count, value], axis=0), field)
            for t in range(tiles):
                out_ref[t, :part, :] += terms[t * part : (t + 1) * part]
            out_ref[0, part:, :] += terms[width:]
            return carry

        lax.fori_loop(0, rows, body, 0)


def lay_basis(basis2, count, value, width, rows, tiles):
    columns = basis2.shape[1]
    block = 32
    strips = columns // LANES
    return pl.pallas_call(
        functools.partial(lay_kernel, rows),
        grid=(width // block,),
        in_specs=[
            pl.BlockSpec((rows, columns), lambda k: (0, 0)),
            pl.BlockSpec((rows, columns), lambda k: (0, 0)),
            *[pl.BlockSpec((block * rows, LANES), lambda k, c=c: (k, c)) for c in range(strips)],
        ],
        out_specs=[
            pl.BlockSpec((rows, block, columns), lambda k: (0, k, 0)),
            pl.BlockSpec((tiles, width // tiles + TAIL, width), lambda k: (0, 0, 0)),
        ],
        out_shape=[
            jax.ShapeDtypeStruct((rows, width, columns), jnp.float32),
            jax.ShapeDtypeStruct((tiles, width // tiles + TAIL, width), jnp.float32),
        ],
        scratch_shapes=[
            pltpu.VMEM((2 * columns, columns), jnp.bfloat16),
            pltpu.VMEM((rows, width, columns), jnp.float32),
        ],
        cost_estimate=pl.CostEstimate(flops=20 * 10**9, bytes_accessed=17 * 10**6, transcendentals=0),
        name="lay_basis",
    )(count, value, *[basis2] * strips)


def prop_kernel(
    place_ref, model_ref, field_ref, low_mine, low_theirs, high_mine, high_theirs, obs_ref,
    out_ref, deal, model, wide, edges, fore, back,
):
    step_id = pl.program_id(0)
    steps = pl.num_programs(0)
    rows, block, columns = field_ref.shape
    ext = rows + 2 * REACH
    width = fore.shape[1]
    half = width // 2
    core, tile, last_tile = place_ref[0], place_ref[1], place_ref[2]
    turn = lax.rem(step_id + core * (steps // 2), steps)

    @pl.when(step_id == 0)
    def _():
        deal[...] = deal_matrix(columns, 3)
        model[...] = jnp.zeros_like(model)
        for f in range(4):
            for r in range(REACH):
                model[f, r : r + 1, :] = low_mine[r, half + f : half + f + 1, :]
                at = REACH + rows + r
                model[f, at : at + 1, :] = high_mine[r, half + f : half + f + 1, :]
            for r in range(rows):
                model[f, REACH + r : REACH + r + 1, :] = model_ref[f, r : r + 1, :]
        tall = model.shape[1]
        together = dealt(model[...].reshape(4 * tall, columns), deal[...])
        lines = lax.broadcasted_iota(jnp.int32, (tall, LANES), 0)
        lanes = lax.broadcasted_iota(jnp.int32, (tall, LANES), 1)
        no_west = jnp.logical_and(tile == 0, lines == REACH)
        no_east = jnp.logical_and(tile == last_tile, lines == REACH + rows - 1)
        diffusion, drift_x, drift_y, sea = (
            strips_of(together[f * tall : (f + 1) * tall]) for f in range(4)
        )
        center, east, west, north, south = [], [], [], [], []
        for c in range(len(sea)):
            center.append(sea[c] * (1.0 - 4.0 * diffusion[c]))
            east.append(jnp.where(no_east, 0.0, sea[c] * (diffusion[c] * (1.0 - drift_x[c]))))
            west.append(jnp.where(no_west, 0.0, sea[c] * (diffusion[c] * (1.0 + drift_x[c]))))
            up = sea[c] * (diffusion[c] * (1.0 - drift_y[c]))
            down = sea[c] * (diffusion[c] * (1.0 + drift_y[c]))
            if c == len(sea) - 1:
                up = jnp.where(lanes == LANES - 1, 0.0, up)
            if c == 0:
                down = jnp.where(lanes == 0, 0.0, down)
            north.append(up)
            south.append(down)
        sets = (
            (center, 0), (east, 0), (west, 0), (north, 0), (south, 0),
            (west, 1), (east, -1), (after(south), 0), (before(north), 0),
        )
        for g, (values, move) in enumerate(sets):
            for r in range(ext):
                if not 0 <= r + move < ext:
                    continue
                line = jnp.concatenate([v[r + move : r + move + 1] for v in values], axis=1)
                wide[g * ext + r] = jnp.broadcast_to(line, (SUB, columns))

    def deal_edges(low, high):
        count = REACH * half
        low_rows = low[:, :half, :].reshape(count, columns)
        high_rows = high[:, :half, :].reshape(count, columns)
        twice = deal[: 2 * columns, :]
        edges[:REACH] = dealt(low_rows, twice).reshape(REACH, half, columns)
        edges[REACH:] = dealt(high_rows, twice).reshape(REACH, half, columns)

    @pl.when(step_id == 0)
    def _():
        deal_edges(low_mine, high_mine)

    @pl.when(step_id == steps // 2)
    def _():
        deal_edges(low_theirs, high_theirs)

    def one(kt, carry):
        near = pl.ds(pl.multiple_of(kt * SUB, SUB), SUB)
        edge = pl.ds(pl.multiple_of(lax.rem(step_id, steps // 2) * block + kt * SUB, SUB), SUB)
        store = pl.ds(pl.multiple_of(turn * block + kt * SUB, SUB), SUB)

        def start(i):
            if i < 0:
                return strips_of(edges[i + REACH, edge, :])
            if i >= rows:
                return strips_of(edges[i - rows + REACH, edge, :])
            return strips_of(field_ref[i, near, :])

        for target, sets in ((fore, (0, 1, 2, 3, 4)), (back, (0, 5, 6, 7, 8))):
            levels = [{} for _ in range(REACH + 1)]
            for lead in range(-REACH, rows + REACH):
                levels[0][lead] = start(lead)
                for s in range(1, REACH + 1):
                    i = lead - s
                    if -REACH + s <= i < rows + REACH - s:
                        prev = levels[s - 1]
                        gains = [wide[g * ext + i + REACH] for g in sets]
                        shifted = (
                            prev[i], prev[i + 1], prev[i - 1], after(prev[i]), before(prev[i])
                        )
                        levels[s][i] = []
                        for c in range(columns // LANES):
                            terms = [
                                gain[:, c * LANES : (c + 1) * LANES] * value[c]
                                for gain, value in zip(gains, shifted)
                            ]
                            levels[s][i].append(
                                (terms[0] + (terms[1] + terms[2])) + (terms[3] + terms[4])
                            )
                i = lead - REACH
                if 0 <= i < rows:
                    target[i, store, :] = jnp.concatenate(levels[REACH][i], axis=1)
        return carry

    lax.fori_loop(0, block // SUB, one, 0)

    @pl.when(step_id == steps - 1)
    def _():
        tiles = out_ref.shape[0]
        part = width // tiles
        out_ref[:, :part, :] = jnp.zeros_like(out_ref[:, :part, :])
        out_ref[:, part:, :] = obs_ref[...]

        def body(i, carry):
            terms = dot3(back[i], fore[i])
            for t in range(tiles):
                out_ref[t, :part, :] += terms[t * part : (t + 1) * part]
            return carry

        lax.fori_loop(0, rows, body, 0)


def prop_terms(place, model, field, edges, obs):
    rows, width, columns = field.shape
    block = 32
    steps = width // block
    ext = rows + 2 * REACH
    vmem = pl.BlockSpec(memory_space=pltpu.VMEM)
    tiles, lines, _ = obs.shape
    total = (tiles, width // tiles + lines, width)
    return pl.pallas_call(
        prop_kernel,
        grid_spec=pltpu.PrefetchScalarGridSpec(
            num_scalar_prefetch=1,
            grid=(steps,),
            in_specs=[
                vmem,
                pl.BlockSpec(
                    (rows, block, columns),
                    lambda k, place: (0, lax.rem(k + place[0] * (steps // 2), steps), 0),
                ),
                vmem,
                vmem,
                vmem,
                vmem,
                vmem,
            ],
            out_specs=pl.BlockSpec(total, lambda k, place: (0, 0, 0)),
            scratch_shapes=[
                pltpu.VMEM((3 * columns, columns), jnp.bfloat16),
                pltpu.VMEM((4, -(-ext // SUB) * SUB, columns), jnp.float32),
                pltpu.VMEM((9 * ext, SUB, columns), jnp.float32),
                pltpu.VMEM((2 * REACH, width // 2, columns), jnp.float32),
                pltpu.VMEM((rows, width, columns), jnp.float32),
                pltpu.VMEM((rows, width, columns), jnp.float32),
            ],
        ),
        out_shape=jax.ShapeDtypeStruct(total, jnp.float32),
        cost_estimate=pl.CostEstimate(flops=35 * 10**9, bytes_accessed=12 * 10**6, transcendentals=0),
        name="prop_terms",
    )(place, model, field, *edges, obs)


def eye_mask(width):
    row = lax.broadcasted_iota(jnp.int32, (width, width), 0)
    col = lax.broadcasted_iota(jnp.int32, (width, width), 1)
    return row, col


def product(left, right, passes):
    if passes == 1:
        return jnp.dot(
            left.astype(jnp.bfloat16),
            right.astype(jnp.bfloat16),
            preferred_element_type=jnp.float32,
        )
    if passes == 3:
        return dot(left, right)
    return jnp.dot(
        left, right, precision=lax.Precision.HIGHEST, preferred_element_type=jnp.float32
    )


def inverses(mats):
    width = mats[0].shape[0]
    row, col = eye_mask(width)
    identity = jnp.where(row == col, 1.0, 0.0).astype(jnp.float32)
    found = []
    error = jnp.float32(0.0)
    for mat in mats:
        bound = jnp.max(jnp.sum(jnp.abs(mat), axis=0, keepdims=True), axis=1, keepdims=True)
        trace = jnp.sum(jnp.sum(identity * mat, axis=0, keepdims=True), axis=1, keepdims=True)
        square = jnp.sum(jnp.sum(mat * mat, axis=0, keepdims=True), axis=1, keepdims=True)
        scale = jnp.minimum(trace / square, 1.9 / bound)
        rest = identity - scale * mat
        found.append(scale * (identity + rest))
        error = jnp.maximum(error, jnp.sum(rest * rest))

    def stage(state, passes, goal, slowest):
        def more(state):
            turn, error, last = state[0], state[1], state[2]
            going = jnp.logical_and(error > goal, turn < 100)
            return jnp.logical_and(going, jnp.logical_or(error < slowest * last, last == 0.0))

        def improve(state):
            error = jnp.float32(0.0)
            found = []
            for mat, guess in zip(mats, state[3:]):
                rest = identity - product(mat, guess, passes[0])
                found.append(guess + product(guess, rest, passes[1]))
                error = jnp.maximum(error, jnp.sum(rest * rest))
            return (state[0] + 1, error, state[1], *found)

        return lax.while_loop(more, improve, state)

    turn = jnp.int32(0)
    for passes, goal, slowest in (((1, 1), 2.0, 0.5), ((3, 1), 1e-3, 0.5), ((6, 3), 1e-6, 2.0)):
        begin = jnp.maximum(error, 2.0 * goal) if passes[0] == 6 else error
        state = stage((turn, begin, jnp.float32(0.0), *found), passes, goal, slowest)
        turn, error, found = state[0], state[1], state[3:]
    return found


def pair_kernel(
    own_ref, other_ref, both_ref, send_ref, left_ref, right_ref, outer_ref, small_ref
):
    tiles, _, width = own_ref.shape
    part = width // tiles
    group = lax.axis_index("tm")
    core, chip = group & 1, group >> 1
    first = core == 0
    row, col = eye_mask(width)
    identity = jnp.where(row == col, 1.0, 0.0).astype(jnp.float32)

    def ordered(own, other):
        return jnp.where(first, own, other), jnp.where(first, other, own)

    def stacked(ref, at):
        return jnp.concatenate([ref[t, at : at + part, :] for t in range(tiles)], axis=0)

    p_left, p_right = ordered(stacked(own_ref, 0), stacked(other_ref, 0))
    info = ordered(stacked(own_ref, part), stacked(other_ref, part))
    rhs_left, rhs_right = ordered(own_ref[0, 2 * part :, :], other_ref[0, 2 * part :, :])
    square_left = dot(p_left, p_left, (0, 0))
    square_right = dot(p_right, p_right, (0, 0))
    middle = (Q + 2 * RIDGE) * identity + info[0] + Q * square_right
    (back,) = inverses([middle])
    toward_left = dot(p_left, back, (0, 0))
    toward_right = dot(jnp.concatenate([p_right, rhs_left], axis=0), back)
    mid = toward_right[width:]
    toward_right = toward_right[:width]
    by_left = dot(jnp.concatenate([toward_left, mid], axis=0), p_left)
    by_right = dot(jnp.concatenate([toward_left, toward_right, mid], axis=0), p_right, (1, 1))
    upper = Q * square_left + RIDGE * identity - (Q * Q) * by_left[:width]
    cross = -(Q * Q) * by_right[:width]
    lower = (Q + RIDGE) * identity + info[1] - (Q * Q) * by_right[width : 2 * width]
    head = Q * by_left[width:]
    tail = rhs_right + Q * by_right[2 * width :]
    both_ref[1, :width, :] = cross
    left_ref[...] = Q * toward_left
    right_ref[...] = Q * toward_right
    outer_ref[...] = jnp.zeros_like(outer_ref)
    small_ref[...] = jnp.zeros_like(small_ref)
    small_ref[0] = mid
    lines = lax.broadcasted_iota(jnp.int32, (TAIL, width), 0)

    def pack(upper, lower, head, tail):
        lower_diag = jnp.sum(jnp.where(row == col, lower, 0.0), axis=0, keepdims=True)
        both_ref[0, :width, :] = jnp.where(row >= col, upper, lower)
        both_ref[0, width:, :] = jnp.where(lines == 0, lower_diag, jnp.where(lines == 1, head, tail))

    opening, closing = chip == 0, chip == CHIPS - 1
    outer = jnp.logical_or(opening, closing)

    @pl.when(outer)
    def _():
        gone = jnp.where(opening, upper, lower)
        kept = jnp.where(opening, lower, upper)
        joint = jnp.where(opening, cross, cross.T)
        gone_rhs = jnp.where(opening, head, tail)
        kept_rhs = jnp.where(opening, tail, head)
        (gone_back,) = inverses([gone])
        toward = dot(joint, gone_back, (0, 0))
        rest = dot(gone_rhs, gone_back)
        both = dot(jnp.concatenate([toward, rest], axis=0), joint)
        kept = kept - both[:width]
        kept_rhs = kept_rhs - both[width:]
        outer_ref[...] = toward
        small_ref[1] = rest
        pack(kept, kept, kept_rhs, kept_rhs)

    @pl.when(jnp.logical_not(outer))
    def _():
        pack(upper, lower, head, tail)

    both_ref[1, width:, :] = jnp.zeros((TAIL, width), jnp.float32)
    send_ref[...] = jnp.where(first, both_ref[0], both_ref[1])


def merge_pair(own, other):
    width = own.shape[2]
    vmem = pl.BlockSpec(memory_space=pltpu.VMEM)
    block = pltpu.VMEM((width, width), jnp.float32)
    return pl.pallas_call(
        pair_kernel,
        in_specs=[vmem] * 2,
        out_specs=[vmem] * 6,
        out_shape=[
            pltpu.VMEM((2, width + TAIL, width), jnp.float32),
            pltpu.VMEM((width + TAIL, width), jnp.float32),
            block,
            block,
            block,
            pltpu.VMEM((2, TAIL, width), jnp.float32),
        ],
        name="merge_pair",
    )(own, other)


def chain_kernel(
    both_ref, m_prev, o_prev, m_next, o_next, m_far, o_far,
    left_ref, right_ref, outer_ref, small_ref,
    basis_ref, coeff_ref, end_ref, blocks, basis, weight, sem,
):
    fetch = pltpu.make_async_copy(basis_ref, basis, sem)
    fetch.start()
    group = lax.axis_index("tm")
    core, chip = group & 1, group >> 1
    width = both_ref.shape[2]
    row, col = eye_mask(width)
    blocks[chip] = both_ref[...]
    for mine, theirs, move in ((m_prev, o_prev, 3), (m_next, o_next, 1), (m_far, o_far, 2)):
        at = lax.rem(chip + move, CHIPS)
        blocks[at, core] = mine[...]
        blocks[at, 1 - core] = theirs[...]
    upper, lower, head, tail = [], [], [], []
    for c in range(CHIPS):
        packed = blocks[c, 0, :width, :]
        turned = packed.T
        small = blocks[c, 0, width:, :]
        upper.append(jnp.where(row >= col, packed, turned))
        off = jnp.where(row < col, packed, turned)
        lower.append(jnp.where(row == col, jnp.broadcast_to(small[0:1], (width, width)), off))
        head.append(jnp.broadcast_to(small[1:2], (TAIL, width)))
        tail.append(jnp.broadcast_to(small[2:3], (TAIL, width)))
    cross1, cross2 = blocks[1, 1, :width, :], blocks[2, 1, :width, :]
    rhs1, rhs2, rhs3 = (tail[c] + head[c + 1] for c in range(3))
    inv1, inv3 = inverses([lower[0] + upper[1], lower[2] + upper[3]])
    toward1 = dot(cross1, inv1, (0, 0))
    toward3 = dot(cross2, inv3)
    z1, z3 = dot(rhs1, inv1), dot(rhs3, inv3)
    by1 = dot(jnp.concatenate([toward1, z1], axis=0), cross1)
    by3 = dot(jnp.concatenate([toward3, z3], axis=0), cross2, (1, 1))
    (inv2,) = inverses([lower[1] + upper[2] - by1[:width] - by3[:width]])
    y2 = dot(rhs2 - by1[width:] - by3[width:], inv2)
    y1 = z1 - dot(y2, toward1)
    y3 = z3 - dot(y2, toward3)
    opening = chip == 0
    y_outer = small_ref[1] - dot(jnp.where(opening, y1, y3), outer_ref[...])
    begin = jnp.where(
        opening, y_outer, jnp.where(chip == 1, y1, jnp.where(chip == 2, y2, y3))
    )
    finish = jnp.where(
        opening, y1, jnp.where(chip == 1, y2, jnp.where(chip == 2, y3, y_outer))
    )
    inner = small_ref[0] + dot(begin, left_ref[...]) + dot(finish, right_ref[...])
    first = core == 0
    start = jnp.where(first, begin, inner)
    end = jnp.where(first, inner, finish)
    coeff_ref[0, 0:1, :] = start[0:1]
    coeff_ref[0, 1:2, :] = end[0:1]
    weight[...] = jnp.concatenate([end] * (LANES // TAIL), axis=0).T
    rows, columns = end_ref.shape[1:]
    fetch.wait()

    def add(k, total):
        line = basis[pl.ds(pl.multiple_of(k * rows, rows), rows), :]
        factor = jnp.broadcast_to(weight[pl.ds(k, 1), :], (rows, LANES))
        return total + line * jnp.concatenate([factor] * (columns // LANES), axis=1)

    end_ref[0] = lax.fori_loop(0, width, add, jnp.zeros((rows, columns), jnp.float32), unroll=8)


def solve_chain(both, received, kept, basis2, rows):
    width = both.shape[2]
    columns = basis2.shape[1]
    vmem = pl.BlockSpec(memory_space=pltpu.VMEM)
    return pl.pallas_call(
        chain_kernel,
        in_specs=[vmem] * 11
        + [pl.BlockSpec(memory_space=pltpu.HBM)],
        out_specs=[vmem, vmem],
        out_shape=[
            jax.ShapeDtypeStruct((1, 2, width), jnp.float32),
            jax.ShapeDtypeStruct((1, rows, columns), jnp.float32),
        ],
        scratch_shapes=[
            pltpu.VMEM((CHIPS, 2, width + TAIL, width), jnp.float32),
            pltpu.VMEM(basis2.shape, jnp.float32),
            pltpu.VMEM((width, LANES), jnp.float32),
            pltpu.SemaphoreType.DMA,
        ],
        name="solve_chain",
    )(both, *received, *kept, basis2)


def shift(value, axis, step, wrap):
    size = lax.axis_size(axis)
    pairs = [(i, (i + step) % size) for i in range(size) if wrap or 0 <= i + step < size]
    return lax.ppermute(value, axis, pairs)


def resident(value):
    return pltpu.with_memory_space_constraint(value, pltpu.VMEM)


def swap_core(value):
    return lax.ppermute(value, "tm", [(i, i ^ 1) for i in range(lax.axis_size("tm"))])


def obs_maps(cells, values, rows, columns):
    local = cells - lax.axis_index("tile") * (rows * columns)
    row = local // columns
    col = local & (columns - 1)
    strips = columns // LANES
    col = (col % strips) * LANES + col // strips
    by_row = (row[None, :] == jnp.arange(rows)[:, None]).astype(jnp.float32)
    by_col = (col[:, None] == jnp.arange(columns)[None, :]).astype(jnp.float32)
    both = jnp.concatenate([by_row, by_row * values[None, :]], axis=0)
    maps = jnp.dot(both, by_col, precision=lax.Precision.HIGHEST)
    return maps[:rows], maps[rows:]


def shards(basis, diffusion, drift_x, drift_y, land_sea, obs_cells, obs_values):
    width, rows, columns = basis.shape
    tiles = lax.axis_size("tile")
    group = lax.axis_index("tm")
    core = group & 1
    chip = group >> 1
    basis2 = basis.reshape(width * rows, columns)
    models = (diffusion, drift_x, drift_y, land_sea[None])
    low_send, high_send, model = edge_terms(core[None], models, basis2, width, rows)
    low = shift(low_send, "tile", 1, False)
    high = shift(high_send, "tile", -1, False)
    count, value = obs_maps(obs_cells[0], obs_values[0], rows, columns)
    field, obs = lay_basis(basis2, count, value, width, rows, tiles)
    low, high, obs = lax.optimization_barrier((low, high, obs))
    edges = (low, swap_core(low), high, swap_core(high))
    place = jnp.stack([core, lax.axis_index("tile"), jnp.int32(tiles - 1)])
    terms = prop_terms(place, model, field, edges, obs)

    slices = jnp.sum(lax.all_to_all(terms, "tile", 0, 0, tiled=True), axis=0)
    lines = lax.broadcasted_iota(jnp.int32, slices.shape, 0)
    cells = float(tiles * rows * columns)
    slices = slices * jnp.where(lines < width // tiles, 1.0 / cells, 1.0 / float(NOBS))
    own = lax.all_to_all(jnp.broadcast_to(slices[None], terms.shape), "tile", 0, 0, tiled=True)
    other = swap_core(own)

    both, send, *kept = merge_pair(own, other)
    received = []
    for step in (2, -2, 4):
        mine = shift(send, "tm", step, True)
        received += [resident(mine), resident(swap_core(mine))]
    kept = [resident(value) for value in kept]
    return tuple(solve_chain(resident(both), received, kept, basis2, rows))


def solution(mesh):
    in_specs = (
        P(None, "tile", None),
        P("tm", "tile", None),
        P("tm", "tile", None),
        P("tm", "tile", None),
        P("tile", None),
        P("tm", None),
        P("tm", None),
    )
    out_specs = (P("tm", None, None), P("tm", "tile", None))
    return jax.shard_map(shards, mesh=mesh, in_specs=in_specs, out_specs=out_specs, check_vma=False)
```
